32 devices in a mesh: col: 4 (over y, x), row: 8 (over z, core).
Axes of the slice: x: 2, y: 2, z: 4, core: 2. Of those that a mesh axis runs over, the one named last changes fastest.
Arguments:
- upper_blocks: float32 [4096, 512], P('row', 'col'), may hold values from -40 to 40
- lower_blocks: float32 [4096, 512], P('row', 'col'), may hold values from -40 to 40
Outputs:
- upper_rotated: float32 [4096, 512], P('row', 'col')
- lower_rotated: float32 [4096, 512], P('row', 'col')
The draws below stay inside these ranges and needn't reach their ends.
All inputs are finite; a program needn't handle non-finite values.
Results may differ from the reference program's by a relative error of at most 0.0001.
Values sent between devices are 32-bit elements; how exact they have to be, the bound alone decides.
A program may use at most 64 MiB of HBM per device.

```python
import math
import jax
import jax.numpy as jnp
from jax import lax

BLOCK = 128
ROUNDS = 2
HALF = 512
COLS = 1024
ROWS = 4096
N_COL = 4


def whole_matrix(key):
    base = jax.random.fold_in(key, 11)
    keys = jax.random.split(base, 4)
    noise = jax.random.normal(keys[0], (ROWS, COLS), jnp.float32)
    mixing = jnp.eye(COLS, dtype=jnp.float32) + 0.7 * jax.random.normal(keys[1], (COLS, COLS), jnp.float32) / math.sqrt(COLS)
    mixed = jnp.dot(noise, mixing, precision=lax.Precision.HIGHEST)
    column_scale = jnp.exp(jax.random.uniform(keys[2], (COLS,), jnp.float32, math.log(0.3), math.log(3.0)))
    position = jnp.arange(ROWS, dtype=jnp.float32) / ROWS
    row_scale = jnp.exp(math.log(3.0) * position + jax.random.uniform(keys[3], (ROWS,), jnp.float32, -0.35, 0.35))
    return jnp.clip(mixed * row_scale[:, None] * column_scale[None, :] / 1.7, -40.0, 40.0)


def draw_upper_blocks(key, part):
    return whole_matrix(key)[:, :HALF]


def draw_lower_blocks(key, part):
    return whole_matrix(key)[:, HALF:]


def setup_inputs(seed: int = 0) -> dict:
    splits = jax.random.split(jax.random.key(seed), 3)
    return {
        "upper_blocks": draw_upper_blocks(jax.random.fold_in(splits[2], 71), 0),
        "lower_blocks": draw_lower_blocks(jax.random.fold_in(splits[2], 71), 0),
    }


def couple(cross_gram, upper_norms, lower_norms):
    column_gap = upper_norms[..., :, None] - lower_norms[..., None, :]
    column_sum = upper_norms[..., :, None] + lower_norms[..., None, :]
    return -cross_gram * column_gap / (2.0 * column_gap * column_gap + 0.5 * column_sum * column_sum + 1e-05)

def rotation(coupling):
    identity = jnp.eye(coupling.shape[0], dtype=coupling.dtype)
    outer_gram = jnp.dot(coupling, coupling.T, precision=lax.Precision.HIGHEST)
    inner_gram = jnp.dot(coupling.T, coupling, precision=lax.Precision.HIGHEST)
    left_factor = jnp.linalg.cholesky(identity + outer_gram)
    right_factor = jnp.linalg.cholesky(identity + inner_gram)
    keep_upper = jax.scipy.linalg.cho_solve((left_factor, True), identity - outer_gram)
    upper_to_lower = jax.scipy.linalg.cho_solve((left_factor, True), 2.0 * coupling)
    lower_to_upper = jax.scipy.linalg.cho_solve((right_factor, True), -2.0 * coupling.T)
    keep_lower = jax.scipy.linalg.cho_solve((right_factor, True), identity - inner_gram)
    return (keep_upper, upper_to_lower, lower_to_upper, keep_lower)

def reference(upper_blocks, lower_blocks):
    upper = upper_blocks.reshape(ROWS, N_COL, BLOCK)
    lower = lower_blocks.reshape(ROWS, N_COL, BLOCK)
    highest = lax.Precision.HIGHEST
    for round_index in range(ROUNDS):
        cross_gram = jnp.einsum('mcb,mcd->cbd', upper, lower, precision=highest) / ROWS
        upper_norms = jnp.sum(upper * upper, axis=0) / ROWS
        lower_norms = jnp.sum(lower * lower, axis=0) / ROWS
        coupling = couple(cross_gram, upper_norms, lower_norms)
        keep_upper, upper_to_lower, lower_to_upper, keep_lower = jax.vmap(rotation)(coupling)
        new_upper = jnp.einsum('mcb,cbd->mcd', upper, keep_upper, precision=highest) + jnp.einsum('mcb,cbd->mcd', lower, lower_to_upper, precision=highest)
        new_lower = jnp.einsum('mcb,cbd->mcd', upper, upper_to_lower, precision=highest) + jnp.einsum('mcb,cbd->mcd', lower, keep_lower, precision=highest)
        if round_index + 1 < ROUNDS:
            upper = jnp.roll(new_upper, 1, axis=1)
            lower = jnp.roll(new_lower, -1, axis=1)
        else:
            upper = new_upper
            lower = new_lower
    return (upper.reshape(ROWS, HALF), lower.reshape(ROWS, HALF))
```

```python
import functools

import jax
import jax.numpy as jnp
from jax import lax
from jax.experimental import pallas as pl
from jax.experimental.pallas import tpu as pltpu
from jax.sharding import PartitionSpec as P

ROUNDS = 2
LOADS = 2
SWAPS = 8
EARLY = 1
RELAYS = 4
RELAYS_FIRST = 3
SHIFTS = 4
STORES = 4
MESH = pl.DeviceIdType.MESH
F32 = jnp.float32
BF16 = jnp.bfloat16


def split(x):
    high = x.astype(BF16)
    low = (x - high.astype(F32)).astype(BF16)
    return high, low


def split_three(x):
    high = x.astype(BF16)
    rest = x - high.astype(F32)
    middle = rest.astype(BF16)
    return high, middle, (rest - middle.astype(F32)).astype(BF16)


def fast_dot(a, b):
    return jnp.dot(a, b, preferred_element_type=F32)


def exact_dot(a, b):
    width = b.shape[1]
    (a0, a1, a2), (b0, b1, b2) = split_three(a), split_three(b)
    upper = jnp.concatenate([b0, b1], axis=1)
    lower = jnp.concatenate([b1, b0], axis=1)
    large = fast_dot(jnp.concatenate([a0, a1], axis=1), jnp.concatenate([upper, lower], axis=0))
    small = fast_dot(jnp.concatenate([a0, a2], axis=1), jnp.concatenate([b2, b0], axis=0))
    return large[:, :width] + (large[:, width:] + small)


def wide(b):
    both = jnp.concatenate(split(b), axis=1)
    return jnp.concatenate([both, both], axis=0)


def tall_dot(a, b_wide):
    width = a.shape[1]
    y = fast_dot(jnp.concatenate(split(a), axis=1), b_wide)
    return y[:, :width] + y[:, width:]


def gram(upper, lower):
    width = upper.shape[1]
    left = jnp.concatenate(split(upper), axis=1)
    right = jnp.concatenate(split(lower), axis=1)
    q = lax.dot_general(
        left, right, (((0,), (0,)), ((), ())), preferred_element_type=F32
    )
    return q[:width, :width] + (q[:width, width:] + q[width:, :width])


def identity(width):
    rows = lax.broadcasted_iota(jnp.int32, (width, width), 0)
    lanes = lax.broadcasted_iota(jnp.int32, (width, width), 1)
    return (rows == lanes).astype(F32)


def shrink(spread):
    square = spread * spread
    gain = 2.0 / (2.0 - square)
    return gain, 0.5 * square * gain


def step_count(width):
    square = (width / 4.0) ** 2
    spread = 0.5 * square / (1.0 + 0.5 * square)
    steps = 0
    while spread > 3e-6:
        spread = shrink(spread)[1]
        steps += 1
    return steps


def inverse(p):
    width = p.shape[0]
    eye = identity(width)
    s = exact_dot(p, p.T)
    total = jnp.sum(jnp.sum(p * p, axis=0, keepdims=True), axis=1, keepdims=True)
    total = jnp.broadcast_to(total, (1, width))
    scale = 1.0 / (1.0 + 0.5 * total)
    spread = 0.5 * total * scale
    e = spread * eye - scale * s
    x = None
    steps = step_count(width)
    for step in range(steps):
        gain, spread = shrink(spread)
        if step == 0:
            x = (gain * scale) * (eye + e)
        else:
            x = gain * (x + exact_dot(x, e))
        if step < steps - 1:
            e = gain * exact_dot(e, e) - spread * eye
    return x


def inverse_adaptive(p):
    width = p.shape[0]
    eye = identity(width)
    s = exact_dot(p, p.T)
    bound = 1.0001 * jnp.max(jnp.sum(jnp.abs(s), axis=0, keepdims=True))
    scale = 1.0 / (1.0 + 0.5 * bound)
    spread = 0.5 * bound * scale
    e = spread * eye - scale * s
    gain, spread = shrink(spread)
    x = (gain * scale) * (eye + e)
    squared = exact_dot(e, e)

    def body(state):
        x, squared, gain, spread = state
        e = gain * squared - spread * eye
        gain, spread = shrink(spread)
        return gain * (x + exact_dot(x, e)), exact_dot(e, e), gain, spread

    return lax.while_loop(lambda state: state[3] > 3e-6, body, (x, squared, gain, spread))[0]


def turn(upper, lower, x_wide, p_wide, d):
    v = tall_dot(d, x_wide)
    return v - upper, lower + tall_dot(v, p_wide)


def kernel(
    n_row, n_col, upper_hbm, lower_hbm, work, out_p,
    loaded, swapped, relayed, gram_out, gram_in, line_out, line_in, totals, others,
    swap_send, swap_recv, gram_send, gram_recv, line_send, line_recv,
    pair_send, pair_recv, other_send, other_recv, relay_send, relay_recv,
    shift_send, shift_recv, load_sem, up_sem, down_sem,
):
    depth, width = upper_hbm.shape
    half = width // 2
    n_line = n_row // 2
    row_total = float(depth * n_row)
    row, col = lax.axis_index("row"), lax.axis_index("col")
    core = lax.rem(row, 2)
    chip_row = row - core
    place = chip_row // 2
    partner = chip_row + 1 - core
    odd = lax.rem(col, 2)
    beside = col + 1 - 2 * odd
    ahead = lax.rem(col + 2, n_col)
    behind = lax.rem(col + n_col - 2, n_col)
    shift_to = ahead + odd * (behind - ahead)
    has_prev, has_next = place > 0, place < n_line - 1

    def line_row(k):
        return lax.rem(row + 2 * k, n_row)

    def piece(i, count):
        return pl.ds(i * (depth // count), depth // count)

    loads = []
    for i in range(LOADS):
        rows = piece(i, LOADS)
        for which, ref in enumerate((upper_hbm, lower_hbm)):
            loads.append(pltpu.make_async_copy(ref.at[rows], loaded.at[which, rows], load_sem.at[which, i]))
            loads[-1].start()
    barrier = pltpu.get_barrier_semaphore()

    def greet(r, c):
        pl.semaphore_signal(barrier, inc=1, device_id={"row": r, "col": c}, device_id_type=MESH)

    greeted = [(chip_row, beside), (chip_row + 1, beside), (partner, col)]
    for c in [ahead] + ([] if n_col == 4 else [behind]):
        greeted += [(chip_row, c), (chip_row + 1, c)]
    for r, c in greeted:
        greet(r, c)

    @pl.when(has_prev)
    def _():
        greet(row - 2, col)

    @pl.when(has_next)
    def _():
        greet(row + 2, col)

    pl.semaphore_wait(barrier, len(greeted) + has_prev.astype(jnp.int32) + has_next.astype(jnp.int32))

    def remote(src, dst, send, recv, r, c):
        return pltpu.make_async_remote_copy(
            src_ref=src, dst_ref=dst, send_sem=send, recv_sem=recv,
            device_id={"row": r, "col": c}, device_id_type=MESH,
        )

    pending = []

    def start(copy):
        copy.start()
        pending.append(copy)
        return copy

    def start_swap(i, refs):
        rows = piece(i, SWAPS)
        return [
            start(
                remote(
                    ref.at[rows], swapped.at[which, rows],
                    swap_send.at[which, i], swap_recv.at[which, i], row, beside,
                )
            )
            for which, ref in enumerate(refs)
        ]

    swaps = [start_swap(i, (upper_hbm, lower_hbm)) for i in range(EARLY)]

    def put_statistics(index, g, upper_sums, lower_sums):
        which = lax.broadcasted_iota(jnp.int32, (8, width), 0)
        norms = jnp.where(which == 0, upper_sums, jnp.where(which == 1, lower_sums, 0.0))
        for k in range(2):
            gram_out[index, k, :half, :] = g[k * half : (k + 1) * half]
            gram_out[index, k, half:, :] = norms

    def reduce_line(index, own):
        line_out[index] = own
        copies = []
        for k in range(1, n_line):
            copies.append(
                start(
                    remote(
                        line_out.at[index], line_in.at[index, k - 1],
                        line_send.at[index, k - 1], line_recv.at[index, k - 1], line_row(k), col,
                    )
                )
            )

        def finish_line():
            total = own
            for k in range(1, n_line):
                copies[k - 1].wait_recv()
                total = total + line_in[index, k - 1]
            return total

        return finish_line

    def pair_copy(index):
        return remote(
            totals.at[index, core], totals.at[index, core],
            pair_send.at[index], pair_recv.at[index], partner, col,
        )

    def coupling(both_halves, norm_rows):
        norms = norm_rows / row_total
        a_row, b = norms[:1], norms[1:2]
        a = jnp.broadcast_to(a_row, (width, width)).T
        gap, both = a - b, a + b
        factor = -gap / (2.0 * gap * gap + 0.5 * both * both + 1e-05)
        return (both_halves.reshape(width, width) / row_total) * factor

    def statistics(index, pieces, fetch):
        g, upper_sums, lower_sums = 0.0, 0.0, 0.0
        for i, rows in enumerate(pieces):
            upper, lower = fetch(i, rows)
            g = g + gram(upper, lower)
            upper_sums = upper_sums + jnp.sum(upper * upper, axis=0, keepdims=True)
            lower_sums = lower_sums + jnp.sum(lower * lower, axis=0, keepdims=True)
        put_statistics(index, g, upper_sums, lower_sums)

    def fetch_loaded(i, rows):
        loads[2 * i].wait()
        loads[2 * i + 1].wait()
        return loaded[0, rows, :], loaded[1, rows, :]

    statistics(0, [piece(i, LOADS) for i in range(LOADS)], fetch_loaded)

    for k in range(2):
        start(
            remote(
                gram_out.at[0, k], gram_in.at[core], gram_send.at[k], gram_recv.at[core],
                chip_row + k, beside,
            )
        )
    swaps += [start_swap(i, (loaded.at[0], loaded.at[1])) for i in range(EARLY, SWAPS)]

    for s in range(n_line - 2):
        tell_up = jnp.logical_and(has_next, place > s)
        tell_down = jnp.logical_and(has_prev, place < n_line - 1 - s)

        @pl.when(tell_up)
        def _():
            pl.semaphore_signal(up_sem.at[s], inc=1, device_id={"row": row + 2, "col": col}, device_id_type=MESH)

        @pl.when(tell_down)
        def _():
            pl.semaphore_signal(down_sem.at[s], inc=1, device_id={"row": row - 2, "col": col}, device_id_type=MESH)

        @pl.when(place > s + 1)
        def _():
            pl.semaphore_wait(up_sem.at[s], 1)

        @pl.when(place < n_line - 2 - s)
        def _():
            pl.semaphore_wait(down_sem.at[s], 1)

    for k in range(2):
        remote(
            gram_out.at[0, k], gram_in.at[k], gram_send.at[k], gram_recv.at[k], row, beside
        ).wait_recv()
    finish_line = reduce_line(0, gram_in[0] + gram_in[1])

    relays = []

    def relay(i):
        rows = piece(i, SWAPS)
        for which in range(2):
            swaps[i][which].wait_recv()
            relays.append(
                start(
                    remote(
                        swapped.at[which, rows], relayed.at[which, rows],
                        relay_send.at[which, i], relay_recv.at[which, i], row, shift_to,
                    )
                )
            )

    for i in range(RELAYS_FIRST):
        relay(i)
    totals[0, core] = finish_line()
    own_copy = start(pair_copy(0))
    for k in range(2):
        start(
            remote(
                totals.at[0, core], others.at[core], other_send.at[k], other_recv.at[core],
                chip_row + k, shift_to,
            )
        )
    for i in range(RELAYS_FIRST, RELAYS):
        relay(i)
    own_copy.wait_recv()
    p = coupling(totals[0, :, :half, :], totals[0, 0, half:, :])
    early_rows = pl.ds(0, RELAYS * (depth // SWAPS))
    back = wide(p.T)
    d = swapped[0, early_rows, :] - tall_dot(swapped[1, early_rows, :], back)
    x_wide, p_wide = wide(2.0 * inverse(p)), wide(p)
    upper_slot, lower_slot = 2 - 2 * odd, 1 + odd

    late = depth - RELAYS * (depth // SWAPS)
    shifts = []
    shift_rows = []
    ready = RELAYS
    for i in range(SHIFTS):
        rows = pl.ds(depth - late + i * (late // SHIFTS), late // SHIFTS)
        shift_rows.append(rows)
        while ready * (depth // SWAPS) < depth - late + (i + 1) * (late // SHIFTS):
            swaps[ready][0].wait_recv()
            swaps[ready][1].wait_recv()
            ready += 1
        upper, lower = swapped[0, rows, :], swapped[1, rows, :]
        new_upper, new_lower = turn(upper, lower, x_wide, p_wide, upper - tall_dot(lower, back))
        work[upper_slot, rows, :] = new_upper
        work[lower_slot, rows, :] = new_lower
        shifts.append(
            start(
                remote(
                    work.at[2, rows], work.at[odd, rows], shift_send.at[i], shift_recv.at[i],
                    row, shift_to,
                )
            )
        )
    if RELAYS:
        upper, lower = swapped[0, early_rows, :], swapped[1, early_rows, :]
        new_upper, new_lower = turn(upper, lower, x_wide, p_wide, d)
        work[upper_slot, early_rows, :] = new_upper
        work[lower_slot, early_rows, :] = new_lower
        for k in range(2):
            remote(
                totals.at[0, k], others.at[k], other_send.at[k], other_recv.at[k], row, shift_to
            ).wait_recv()
        p = coupling(others[:, :half, :], others[0, half:, :])
        for copy in relays:
            copy.wait_recv()
        upper, lower = relayed[0], relayed[1]
        d = upper - tall_dot(lower, wide(p.T))
        new_upper, new_lower = turn(upper, lower, wide(2.0 * inverse(p)), wide(p), d)
        work[2 * odd, early_rows, :] = new_upper
        work[2 - odd, early_rows, :] = new_lower

    def fetch_shifted(i, rows):
        if i >= len(pieces) - SHIFTS:
            shifts[i - (len(pieces) - SHIFTS)].wait_recv()
        return work[0, rows, :], work[1, rows, :]

    pieces = ([early_rows] if RELAYS else []) + shift_rows
    statistics(1, pieces, fetch_shifted)
    copy = start(
        remote(gram_out.at[1, 1 - core], gram_in.at[2], gram_send.at[2], gram_recv.at[2], partner, col)
    )
    copy.wait_recv()
    total = reduce_line(1, gram_out[1, core] + gram_in[2])()
    totals[1, core] = total
    copy = start(pair_copy(1))
    copy.wait_recv()
    out_p[...] = coupling(totals[1, :, :half, :], totals[1, 0, half:, :])
    for copy in pending:
        copy.wait_send()


def finish(work, p_ref, out_upper, out_lower, stage, sems):
    depth, width = out_upper.shape
    chunk = depth // STORES
    p = p_ref[...]
    d = work[0] - tall_dot(work[1], wide(p.T))
    p_wide, x_wide = wide(p), wide(2.0 * inverse_adaptive(p))
    copies = []
    for i in range(STORES):
        rows = pl.ds(i * chunk, chunk)
        y = turn(work[0, rows, :], work[1, rows, :], x_wide, p_wide, d[i * chunk : (i + 1) * chunk])
        for which, out in enumerate((out_upper, out_lower)):
            stage[which, rows, :] = y[which]
            copies.append(pltpu.make_async_copy(stage.at[which, rows], out.at[rows], sems.at[which, i]))
            copies[-1].start()
    for copy in copies:
        copy.wait()


def shards(n_row, n_col, upper_blocks, lower_blocks):
    depth, width = upper_blocks.shape
    half = width // 2
    n_line = n_row // 2
    out = jax.ShapeDtypeStruct((depth, width), F32)
    dma = pltpu.SemaphoreType.DMA
    flag = pltpu.SemaphoreType.REGULAR
    work, p = pl.pallas_call(
        functools.partial(kernel, n_row, n_col),
        out_shape=(pltpu.VMEM((3, depth, width), F32), pltpu.VMEM((width, width), F32)),
        in_specs=[pl.BlockSpec(memory_space=pl.ANY)] * 2,
        out_specs=(pl.BlockSpec(memory_space=pltpu.VMEM),) * 2,
        scratch_shapes=[
            pltpu.VMEM((2, depth, width), F32),
            pltpu.VMEM((2, depth, width), F32),
            pltpu.VMEM((2, max(RELAYS, 1) * (depth // SWAPS), width), F32),
            pltpu.VMEM((ROUNDS, 2, half + 8, width), F32),
            pltpu.VMEM((3, half + 8, width), F32),
            pltpu.VMEM((ROUNDS, half + 8, width), F32),
            pltpu.VMEM((ROUNDS, n_line - 1, half + 8, width), F32),
            pltpu.VMEM((ROUNDS, 2, half + 8, width), F32),
            pltpu.VMEM((2, half + 8, width), F32),
            dma((2, SWAPS)),
            dma((2, SWAPS)),
            dma((3,)),
            dma((3,)),
            dma((ROUNDS, n_line - 1)),
            dma((ROUNDS, n_line - 1)),
            dma((ROUNDS,)),
            dma((ROUNDS,)),
            dma((2,)),
            dma((2,)),
            dma((2, max(RELAYS, 1))),
            dma((2, max(RELAYS, 1))),
            dma((SHIFTS,)),
            dma((SHIFTS,)),
            dma((2, LOADS)),
            flag((max(n_line - 2, 1),)),
            flag((max(n_line - 2, 1),)),
        ],
        compiler_params=pltpu.CompilerParams(collective_id=0, has_side_effects=True),
    )(upper_blocks, lower_blocks)
    return pl.pallas_call(
        finish,
        out_shape=(out, out),
        in_specs=[pl.BlockSpec(memory_space=pltpu.VMEM)] * 2,
        out_specs=(pl.BlockSpec(memory_space=pl.ANY),) * 2,
        scratch_shapes=[pltpu.VMEM((2, depth, width), F32), dma((2, STORES))],
    )(*(pltpu.with_memory_space_constraint(x, pltpu.VMEM) for x in (work, p)))


def solution(mesh):
    placed = (P("row", "col"), P("row", "col"))
    return jax.shard_map(
        functools.partial(shards, mesh.shape["row"], mesh.shape["col"]),
        mesh=mesh,
        in_specs=placed,
        out_specs=(P("row", "col"), P("row", "col")),
        check_vma=False,
    )
```

```python
import functools

import jax
import jax.numpy as jnp
from jax import lax
from jax.experimental import pallas as pl
from jax.experimental.pallas import tpu as pltpu
from jax.sharding import PartitionSpec as P

ROUNDS = 2
LOADS = 2
RELAYED = 5
SHIFTS = 3
MOVES = 4
MOVES_FIRST = 4
STORES = 4
MESH = pl.DeviceIdType.MESH
F32 = jnp.float32
BF16 = jnp.bfloat16


def split(x):
    high = x.astype(BF16)
    low = (x - high.astype(F32)).astype(BF16)
    return high, low


def split_three(x):
    high = x.astype(BF16)
    rest = x - high.astype(F32)
    middle = rest.astype(BF16)
    return high, middle, (rest - middle.astype(F32)).astype(BF16)


def fast_dot(a, b):
    return jnp.dot(a, b, preferred_element_type=F32)


def exact_dot(a, b):
    width = b.shape[1]
    (a0, a1, a2), (b0, b1, b2) = split_three(a), split_three(b)
    upper = jnp.concatenate([b0, b1], axis=1)
    lower = jnp.concatenate([b1, b0], axis=1)
    large = fast_dot(jnp.concatenate([a0, a1], axis=1), jnp.concatenate([upper, lower], axis=0))
    small = fast_dot(jnp.concatenate([a0, a2], axis=1), jnp.concatenate([b2, b0], axis=0))
    return large[:, :width] + (large[:, width:] + small)


def wide(b):
    both = jnp.concatenate(split(b), axis=1)
    return jnp.concatenate([both, both], axis=0)


def tall_dot(a, b_wide):
    width = a.shape[1]
    y = fast_dot(jnp.concatenate(split(a), axis=1), b_wide)
    return y[:, :width] + y[:, width:]


def gram(upper, lower):
    width = upper.shape[1]
    left = jnp.concatenate(split(upper), axis=1)
    right = jnp.concatenate(split(lower), axis=1)
    q = lax.dot_general(
        left, right, (((0,), (0,)), ((), ())), preferred_element_type=F32
    )
    return q[:width, :width] + (q[:width, width:] + q[width:, :width])


def identity(width):
    rows = lax.broadcasted_iota(jnp.int32, (width, width), 0)
    lanes = lax.broadcasted_iota(jnp.int32, (width, width), 1)
    return (rows == lanes).astype(F32)


def shrink(spread):
    square = spread * spread
    gain = 2.0 / (2.0 - square)
    return gain, 0.5 * square * gain


def step_count(width):
    square = (width / 4.0) ** 2
    spread = 0.5 * square / (1.0 + 0.5 * square)
    steps = 0
    while spread > 3e-6:
        spread = shrink(spread)[1]
        steps += 1
    return steps


def inverse(p):
    width = p.shape[0]
    eye = identity(width)
    s = exact_dot(p, p.T)
    total = jnp.sum(jnp.sum(p * p, axis=0, keepdims=True), axis=1, keepdims=True)
    total = jnp.broadcast_to(total, (1, width))
    scale = 1.0 / (1.0 + 0.5 * total)
    spread = 0.5 * total * scale
    e = spread * eye - scale * s
    x = None
    steps = step_count(width)
    for step in range(steps):
        gain, spread = shrink(spread)
        if step == 0:
            x = (gain * scale) * (eye + e)
        else:
            x = gain * (x + exact_dot(x, e))
        if step < steps - 1:
            e = gain * exact_dot(e, e) - spread * eye
    return x


def inverse_adaptive(p):
    width = p.shape[0]
    eye = identity(width)
    s = exact_dot(p, p.T)
    bound = 1.0001 * jnp.max(jnp.sum(jnp.abs(s), axis=0, keepdims=True))
    scale = 1.0 / (1.0 + 0.5 * bound)
    spread = 0.5 * bound * scale
    e = spread * eye - scale * s
    gain, spread = shrink(spread)
    x = (gain * scale) * (eye + e)
    squared = exact_dot(e, e)

    def body(state):
        x, squared, gain, spread = state
        e = gain * squared - spread * eye
        gain, spread = shrink(spread)
        return gain * (x + exact_dot(x, e)), exact_dot(e, e), gain, spread

    return lax.while_loop(lambda state: state[3] > 3e-6, body, (x, squared, gain, spread))[0]


def turn(upper, lower, x_wide, p_wide, d):
    v = tall_dot(d, x_wide)
    return v - upper, lower + tall_dot(v, p_wide)


def kernel(
    n_row, n_col, upper_hbm, lower_hbm, work, out_p,
    loaded, relayed, home, gram_out, gram_in, line_out, line_in, totals, others,
    gram_send, gram_recv, line_send, line_recv,
    pair_send, pair_recv, other_send, other_recv, relay_send, relay_recv,
    shift_send, shift_recv, move_send, move_recv, load_sem, up_sem, down_sem,
):
    depth, width = upper_hbm.shape
    half = width // 2
    n_line = n_row // 2
    row_total = float(depth * n_row)
    row, col = lax.axis_index("row"), lax.axis_index("col")
    core = lax.rem(row, 2)
    chip_row = row - core
    place = chip_row // 2
    partner = chip_row + 1 - core
    even = 1 - lax.rem(col, 2)
    beside = col - 1 + 2 * even
    ahead = lax.rem(col + 2, n_col)
    behind = lax.rem(col + n_col - 2, n_col)
    shift_to = ahead + even * (behind - ahead)
    has_prev, has_next = place > 0, place < n_line - 1
    early = RELAYED * (depth // 8)
    early_rows = pl.ds(0, early)

    def line_row(k):
        return lax.rem(row + 2 * k, n_row)

    def piece(i, count, first=0, last=None):
        size = ((depth if last is None else last) - first) // count
        return pl.ds(first + i * size, size)

    loads = []
    for i in range(LOADS):
        rows = piece(i, LOADS)
        for which, ref in enumerate((upper_hbm, lower_hbm)):
            loads.append(pltpu.make_async_copy(ref.at[rows], loaded.at[which, rows], load_sem.at[which, i]))
            loads[-1].start()
    barrier = pltpu.get_barrier_semaphore()

    def greet(r, c):
        pl.semaphore_signal(barrier, inc=1, device_id={"row": r, "col": c}, device_id_type=MESH)

    greeted = [(chip_row, beside), (chip_row + 1, beside), (partner, col)]
    for c in [ahead] + ([] if n_col == 4 else [behind]):
        greeted += [(chip_row, c), (chip_row + 1, c)]
    for r, c in greeted:
        greet(r, c)

    @pl.when(has_prev)
    def _():
        greet(row - 2, col)

    @pl.when(has_next)
    def _():
        greet(row + 2, col)

    pl.semaphore_wait(barrier, len(greeted) + has_prev.astype(jnp.int32) + has_next.astype(jnp.int32))

    def remote(src, dst, send, recv, r, c):
        return pltpu.make_async_remote_copy(
            src_ref=src, dst_ref=dst, send_sem=send, recv_sem=recv,
            device_id={"row": r, "col": c}, device_id_type=MESH,
        )

    pending = []

    def start(copy):
        copy.start()
        pending.append(copy)
        return copy

    relays = [
        start(
            remote(
                ref.at[early_rows], relayed.at[which], relay_send.at[which], relay_recv.at[which], row, shift_to
            )
        )
        for which, ref in enumerate((upper_hbm, lower_hbm))
    ]

    def put_statistics(index, g, upper_sums, lower_sums):
        which = lax.broadcasted_iota(jnp.int32, (8, width), 0)
        norms = jnp.where(which == 0, upper_sums, jnp.where(which == 1, lower_sums, 0.0))
        for k in range(2):
            gram_out[index, k, :half, :] = g[k * half : (k + 1) * half]
            gram_out[index, k, half:, :] = norms

    def reduce_line(index, own):
        line_out[index] = own
        copies = []
        for k in range(1, n_line):
            copies.append(
                start(
                    remote(
                        line_out.at[index], line_in.at[index, k - 1],
                        line_send.at[index, k - 1], line_recv.at[index, k - 1], line_row(k), col,
                    )
                )
            )
        total = own
        for k in range(1, n_line):
            copies[k - 1].wait_recv()
            total = total + line_in[index, k - 1]
        totals[index, core] = total
        return start(
            remote(
                totals.at[index, core], totals.at[index, core],
                pair_send.at[index], pair_recv.at[index], partner, col,
            )
        )

    def coupling(both_halves, norm_rows):
        norms = norm_rows / row_total
        a_row, b = norms[:1], norms[1:2]
        a = jnp.broadcast_to(a_row, (width, width)).T
        gap, both = a - b, a + b
        factor = -gap / (2.0 * gap * gap + 0.5 * both * both + 1e-05)
        return (both_halves.reshape(width, width) / row_total) * factor

    def statistics(index, pieces, fetch):
        g, upper_sums, lower_sums = 0.0, 0.0, 0.0
        for i, rows in enumerate(pieces):
            upper, lower = fetch(i, rows)
            g = g + gram(upper, lower)
            upper_sums = upper_sums + jnp.sum(upper * upper, axis=0, keepdims=True)
            lower_sums = lower_sums + jnp.sum(lower * lower, axis=0, keepdims=True)
        put_statistics(index, g, upper_sums, lower_sums)

    def fetch_loaded(i, rows):
        loads[2 * i].wait()
        loads[2 * i + 1].wait()
        return loaded[0, rows, :], loaded[1, rows, :]

    statistics(0, [piece(i, LOADS) for i in range(LOADS)], fetch_loaded)
    copy = start(
        remote(gram_out.at[0, 1 - core], gram_in.at[2], gram_send.at[2], gram_recv.at[2], partner, col)
    )

    for s in range(n_line - 2):

        @pl.when(jnp.logical_and(has_next, place > s))
        def _():
            pl.semaphore_signal(up_sem.at[s], inc=1, device_id={"row": row + 2, "col": col}, device_id_type=MESH)

        @pl.when(jnp.logical_and(has_prev, place < n_line - 1 - s))
        def _():
            pl.semaphore_signal(down_sem.at[s], inc=1, device_id={"row": row - 2, "col": col}, device_id_type=MESH)

        @pl.when(place > s + 1)
        def _():
            pl.semaphore_wait(up_sem.at[s], 1)

        @pl.when(place < n_line - 2 - s)
        def _():
            pl.semaphore_wait(down_sem.at[s], 1)

    copy.wait_recv()
    own_copy = reduce_line(0, gram_out[0, core] + gram_in[2])
    for k in range(2):
        start(
            remote(
                totals.at[0, core], others.at[core], other_send.at[k], other_recv.at[core],
                chip_row + k, shift_to,
            )
        )
    own_copy.wait_recv()
    p = coupling(totals[0, :, :half, :], totals[0, 0, half:, :])
    upper, lower = loaded[0], loaded[1]
    d = upper - tall_dot(lower, wide(p.T))
    x_wide, p_wide = wide(2.0 * inverse(p)), wide(p)
    upper_slot, lower_slot = 2 - 2 * even, 1 + even
    kept, received = 1 - even, even

    def place_turned(rows, size):
        new_upper, new_lower = turn(
            loaded[0, rows, :], loaded[1, rows, :], x_wide, p_wide, d[rows.start : rows.start + size]
        )
        home[upper_slot, rows, :] = new_upper
        home[lower_slot, rows, :] = new_lower

    moves = []

    def move(slot, rows):
        i = len(moves)
        moves.append(
            start(
                remote(
                    home.at[slot, rows], work.at[slot, rows], move_send.at[i], move_recv.at[i], row, beside
                )
            )
        )

    shifts = []
    shift_rows = [piece(i, SHIFTS, early) for i in range(SHIFTS)]
    for i, rows in enumerate(shift_rows):
        place_turned(rows, rows.size)
        shifts.append(
            start(
                remote(
                    home.at[2, rows], home.at[received, rows], shift_send.at[i], shift_recv.at[i],
                    row, shift_to,
                )
            )
        )
    place_turned(early_rows, early)
    for i in range(MOVES_FIRST):
        move(kept, piece(i, MOVES))
    for k in range(2):
        remote(
            totals.at[0, k], others.at[k], other_send.at[k], other_recv.at[k], row, shift_to
        ).wait_recv()
    p = coupling(others[:, :half, :], others[0, half:, :])
    for copy in relays:
        copy.wait_recv()
    upper, lower = relayed[0], relayed[1]
    d = upper - tall_dot(lower, wide(p.T))
    new_upper, new_lower = turn(upper, lower, wide(2.0 * inverse(p)), wide(p), d)
    home[2 * even, early_rows, :] = new_upper
    home[2 - even, early_rows, :] = new_lower

    def fetch_shifted(i, rows):
        if i > 0:
            shifts[i - 1].wait_recv()
        return home[0, rows, :], home[1, rows, :]

    statistics(1, [early_rows] + shift_rows, fetch_shifted)
    copy = start(
        remote(gram_out.at[1, 1 - core], gram_in.at[2], gram_send.at[0], gram_recv.at[0], partner, col)
    )
    copy.wait_recv()
    gram_in[0] = gram_out[1, core] + gram_in[2]
    crossed = start(remote(gram_in.at[0], gram_in.at[1], gram_send.at[1], gram_recv.at[1], row, beside))
    for i in range(MOVES_FIRST, MOVES):
        move(kept, piece(i, MOVES))
    for i in range(MOVES):
        move(received, piece(i, MOVES))
    crossed.wait_recv()
    reduce_line(1, gram_in[1]).wait_recv()
    out_p[...] = coupling(totals[1, :, :half, :], totals[1, 0, half:, :])
    incoming = [(received, i) for i in range(MOVES_FIRST)] + [(received, i) for i in range(MOVES_FIRST, MOVES)]
    incoming += [(kept, i) for i in range(MOVES)]
    for i, (slot, k) in enumerate(incoming):
        rows = piece(k, MOVES)
        remote(
            home.at[slot, rows], work.at[slot, rows], move_send.at[i], move_recv.at[i], row, beside
        ).wait_recv()
    for copy in pending:
        copy.wait_send()


def finish(work, p_ref, out_upper, out_lower, stage, sems):
    depth, width = out_upper.shape
    chunk = depth // STORES
    p = p_ref[...]
    d = work[0] - tall_dot(work[1], wide(p.T))
    p_wide, x_wide = wide(p), wide(2.0 * inverse_adaptive(p))
    copies = []
    for i in range(STORES):
        rows = pl.ds(i * chunk, chunk)
        y = turn(work[0, rows, :], work[1, rows, :], x_wide, p_wide, d[i * chunk : (i + 1) * chunk])
        for which, out in enumerate((out_upper, out_lower)):
            stage[which, rows, :] = y[which]
            copies.append(pltpu.make_async_copy(stage.at[which, rows], out.at[rows], sems.at[which, i]))
            copies[-1].start()
    for copy in copies:
        copy.wait()


def shards(n_row, n_col, upper_blocks, lower_blocks):
    depth, width = upper_blocks.shape
    half = width // 2
    n_line = n_row // 2
    out = jax.ShapeDtypeStruct((depth, width), F32)
    dma = pltpu.SemaphoreType.DMA
    flag = pltpu.SemaphoreType.REGULAR
    work, p = pl.pallas_call(
        functools.partial(kernel, n_row, n_col),
        out_shape=(pltpu.VMEM((2, depth, width), F32), pltpu.VMEM((width, width), F32)),
        in_specs=[pl.BlockSpec(memory_space=pl.ANY)] * 2,
        out_specs=(pl.BlockSpec(memory_space=pltpu.VMEM),) * 2,
        scratch_shapes=[
            pltpu.VMEM((2, depth, width), F32),
            pltpu.VMEM((2, RELAYED * (depth // 8), width), F32),
            pltpu.VMEM((3, depth, width), F32),
            pltpu.VMEM((ROUNDS, 2, half + 8, width), F32),
            pltpu.VMEM((3, half + 8, width), F32),
            pltpu.VMEM((ROUNDS, half + 8, width), F32),
            pltpu.VMEM((ROUNDS, n_line - 1, half + 8, width), F32),
            pltpu.VMEM((ROUNDS, 2, half + 8, width), F32),
            pltpu.VMEM((2, half + 8, width), F32),
            dma((3,)),
            dma((3,)),
            dma((ROUNDS, n_line - 1)),
            dma((ROUNDS, n_line - 1)),
            dma((ROUNDS,)),
            dma((ROUNDS,)),
            dma((2,)),
            dma((2,)),
            dma((2,)),
            dma((2,)),
            dma((SHIFTS,)),
            dma((SHIFTS,)),
            dma((2 * MOVES,)),
            dma((2 * MOVES,)),
            dma((2, LOADS)),
            flag((max(n_line - 2, 1),)),
            flag((max(n_line - 2, 1),)),
        ],
        compiler_params=pltpu.CompilerParams(collective_id=0, has_side_effects=True),
    )(upper_blocks, lower_blocks)
    return pl.pallas_call(
        finish,
        out_shape=(out, out),
        in_specs=[pl.BlockSpec(memory_space=pltpu.VMEM)] * 2,
        out_specs=(pl.BlockSpec(memory_space=pl.ANY),) * 2,
        scratch_shapes=[pltpu.VMEM((2, depth, width), F32), dma((2, STORES))],
    )(*(pltpu.with_memory_space_constraint(x, pltpu.VMEM) for x in (work, p)))


def solution(mesh):
    placed = (P("row", "col"), P("row", "col"))
    return jax.shard_map(
        functools.partial(shards, mesh.shape["row"], mesh.shape["col"]),
        mesh=mesh,
        in_specs=placed,
        out_specs=(P("row", "col"), P("row", "col")),
        check_vma=False,
    )
```

```python
import functools

import jax
import jax.numpy as jnp
from jax import lax
from jax.experimental import pallas as pl
from jax.experimental.pallas import tpu as pltpu
from jax.sharding import PartitionSpec as P

ROUNDS = 2
LOADS = 2
RELAYED = 5
RAW_FROM = 2
RECEIVED_FIRST = 3
SHIFTS = 1
MIDDLE = 4
EXACT_ABOVE = 1.0
STORES = 4
MESH = pl.DeviceIdType.MESH
F32 = jnp.float32
BF16 = jnp.bfloat16


def split(x):
    high = x.astype(BF16)
    low = (x - high.astype(F32)).astype(BF16)
    return high, low


def split_three(x):
    high = x.astype(BF16)
    rest = x - high.astype(F32)
    middle = rest.astype(BF16)
    return high, middle, (rest - middle.astype(F32)).astype(BF16)


def fast_dot(a, b):
    return jnp.dot(a, b, preferred_element_type=F32)


def exact_dot(a, b):
    width = b.shape[1]
    (a0, a1, a2), (b0, b1, b2) = split_three(a), split_three(b)
    upper = jnp.concatenate([b0, b1], axis=1)
    lower = jnp.concatenate([b1, b0], axis=1)
    large = fast_dot(jnp.concatenate([a0, a1], axis=1), jnp.concatenate([upper, lower], axis=0))
    small = fast_dot(jnp.concatenate([a0, a2], axis=1), jnp.concatenate([b2, b0], axis=0))
    return large[:, :width] + (large[:, width:] + small)


def wide(b):
    both = jnp.concatenate(split(b), axis=1)
    return jnp.concatenate([both, both], axis=0)


def tall_dot(a, b_wide):
    width = a.shape[1]
    y = fast_dot(jnp.concatenate(split(a), axis=1), b_wide)
    return y[:, :width] + y[:, width:]


def gram(upper, lower):
    width = upper.shape[1]
    left = jnp.concatenate(split(upper), axis=1)
    right = jnp.concatenate(split(lower), axis=1)
    q = lax.dot_general(
        left, right, (((0,), (0,)), ((), ())), preferred_element_type=F32
    )
    return q[:width, :width] + (q[:width, width:] + q[width:, :width])


def identity(width):
    rows = lax.broadcasted_iota(jnp.int32, (width, width), 0)
    lanes = lax.broadcasted_iota(jnp.int32, (width, width), 1)
    return (rows == lanes).astype(F32)


def shrink(spread):
    square = spread * spread
    gain = 2.0 / (2.0 - square)
    return gain, 0.5 * square * gain


def step_count(width):
    square = (width / 4.0) ** 2
    spread = 0.5 * square / (1.0 + 0.5 * square)
    steps = 0
    while spread > 1e-3:
        spread = shrink(spread)[1]
        steps += 1
    return steps


def quick_dot(a, b):
    return tall_dot(a, wide(b))


def correct(s, x):
    e = (identity(x.shape[0]) - x) - exact_dot(s, x)
    return x + quick_dot(x, e)


def inverse_first(p, middle):
    width = p.shape[0]
    eye = identity(width)
    s = exact_dot(p, p.T)
    total = jnp.sum(jnp.sum(p * p, axis=0, keepdims=True), axis=1, keepdims=True)
    total = jnp.broadcast_to(total, (1, width))
    scale = 1.0 / (1.0 + 0.5 * total)
    spread = 0.5 * total * scale
    e = spread * eye - scale * s
    gain, spread = shrink(spread)
    x = (gain * scale) * (eye + e)
    e = gain * quick_dot(e, e) - spread * eye
    return inverse_steps((s, x, e, spread), 1, middle, step_count(width))


def inverse_steps(state, first, last, steps):
    s, x, e, spread = state
    for step in range(first, last):
        gain, spread = shrink(spread)
        x = gain * (x + quick_dot(x, e))
        if step < steps - 1:
            e = gain * quick_dot(e, e) - spread * identity(x.shape[0])
    return s, x, e, spread


def inverse_last(state, middle):
    steps = step_count(state[0].shape[0])
    s, x, _, _ = inverse_steps(state, middle, steps, steps)
    return correct(s, x)


def inverse(p):
    return inverse_last(inverse_first(p, 1), 1)


def inverse_adaptive(p):
    width = p.shape[0]
    eye = identity(width)
    s = exact_dot(p, p.T)
    bound = 1.0001 * jnp.max(jnp.sum(jnp.abs(s), axis=0, keepdims=True))
    scale = 1.0 / (1.0 + 0.5 * bound)
    spread = 0.5 * bound * scale
    e = spread * eye - scale * s
    gain, spread = shrink(spread)
    x = (gain * scale) * (eye + e)
    squared = exact_dot(e, e)

    def body(state):
        x, squared, gain, spread = state
        e = gain * squared - spread * eye
        gain, spread = shrink(spread)
        return gain * (x + exact_dot(x, e)), exact_dot(e, e), gain, spread

    x = lax.while_loop(lambda state: state[3] > 3e-6, body, (x, squared, gain, spread))[0]
    return lax.cond(bound > EXACT_ABOVE, lambda: correct(s, x), lambda: x)


def turn(upper, lower, x_wide, p_wide, d):
    v = tall_dot(d, x_wide)
    return v - upper, lower + tall_dot(v, p_wide)


def kernel(
    n_row, n_col, upper_hbm, lower_hbm, work, out_p,
    loaded, relayed, swapped, home, gram_out, gram_in, line_out, line_in, cross_in, totals, others, besides,
    gram_send, gram_recv, line_send, line_recv, cross_send, cross_recv,
    pair_send, pair_recv, other_send, other_recv, beside_send, beside_recv,
    relay_send, relay_recv, swap_send, swap_recv, shift_send, shift_recv, carry_send, carry_recv, move_send, move_recv, load_sem, up_sem, down_sem,
):
    depth, width = upper_hbm.shape
    half = width // 2
    n_line = n_row // 2
    row_total = float(depth * n_row)
    row, col = lax.axis_index("row"), lax.axis_index("col")
    core = lax.rem(row, 2)
    chip_row = row - core
    place = chip_row // 2
    partner = chip_row + 1 - core
    odd = lax.rem(col, 2)
    even = 1 - odd
    beside = col + 1 - 2 * odd
    ahead = lax.rem(col + 2, n_col)
    behind = lax.rem(col + n_col - 2, n_col)
    shift_to = ahead + even * (behind - ahead)
    carry_to = ahead + odd * (behind - ahead)
    has_prev, has_next = place > 0, place < n_line - 1
    early = RELAYED * (depth // 8)
    early_rows = pl.ds(0, early)

    def line_row(k):
        return lax.rem(row + 2 * k, n_row)

    def piece(i, count, first=0, last=None):
        size = ((depth if last is None else last) - first) // count
        return pl.ds(first + i * size, size)

    loads = []
    for i in range(LOADS):
        rows = piece(i, LOADS)
        for which, ref in enumerate((upper_hbm, lower_hbm)):
            loads.append(pltpu.make_async_copy(ref.at[rows], loaded.at[which, rows], load_sem.at[which, i]))
            loads[-1].start()
    barrier = pltpu.get_barrier_semaphore()

    def greet(r, c):
        pl.semaphore_signal(barrier, inc=1, device_id={"row": r, "col": c}, device_id_type=MESH)

    greeted = [(chip_row, beside), (chip_row + 1, beside), (partner, col)]
    for c in [ahead] + ([] if n_col == 4 else [behind]):
        greeted += [(chip_row, c), (chip_row + 1, c)]
    for r, c in greeted:
        greet(r, c)

    @pl.when(has_prev)
    def _():
        greet(row - 2, col)

    @pl.when(has_next)
    def _():
        greet(row + 2, col)

    pl.semaphore_wait(barrier, len(greeted) + has_prev.astype(jnp.int32) + has_next.astype(jnp.int32))

    def remote(src, dst, send, recv, r, c):
        return pltpu.make_async_remote_copy(
            src_ref=src, dst_ref=dst, send_sem=send, recv_sem=recv,
            device_id={"row": r, "col": c}, device_id_type=MESH,
        )

    pending = []

    def start(copy):
        copy.start()
        pending.append(copy)
        return copy

    def send_raw(i, first, last, dst, send, recv, c):
        rows = pl.ds(first * (depth // 8), (last - first) * (depth // 8))
        return [
            start(remote(ref.at[rows], dst.at[which, rows], send.at[which, i], recv.at[which, i], row, c))
            for which, ref in enumerate((upper_hbm, lower_hbm))
        ]

    def relay(i, first, last):
        return send_raw(i, first, last, relayed, relay_send, relay_recv, shift_to)

    def swap(i, first, last):
        return send_raw(i, first, last, swapped, swap_send, swap_recv, beside)

    relays = relay(0, 0, RELAYED)
    swaps = swap(0, RAW_FROM, 8)

    def put_statistics(index, g, upper_sums, lower_sums):
        which = lax.broadcasted_iota(jnp.int32, (8, width), 0)
        norms = jnp.where(which == 0, upper_sums, jnp.where(which == 1, lower_sums, 0.0))
        for k in range(2):
            gram_out[index, k, :half, :] = g[k * half : (k + 1) * half]
            gram_out[index, k, half:, :] = norms

    def share(index, total):
        totals[index, core] = total
        return start(
            remote(
                totals.at[index, core], totals.at[index, core],
                pair_send.at[index], pair_recv.at[index], partner, col,
            )
        )

    def reduce_line(own):
        line_out[0] = own
        copies = []
        for k in range(1, n_line):
            copies.append(
                start(
                    remote(
                        line_out.at[0], line_in.at[k - 1],
                        line_send.at[k - 1], line_recv.at[k - 1], line_row(k), col,
                    )
                )
            )
        total = own
        for k in range(1, n_line):
            copies[k - 1].wait_recv()
            total = total + line_in[k - 1]
        return total

    def coupling(both_halves, norm_rows):
        norms = norm_rows / row_total
        a_row, b = norms[:1], norms[1:2]
        a = jnp.broadcast_to(a_row, (width, width)).T
        gap, both = a - b, a + b
        factor = -gap / (2.0 * gap * gap + 0.5 * both * both + 1e-05)
        return (both_halves.reshape(width, width) / row_total) * factor

    def statistics(index, pieces, fetch):
        g, upper_sums, lower_sums = 0.0, 0.0, 0.0
        for i, rows in enumerate(pieces):
            upper, lower = fetch(i, rows)
            g = g + gram(upper, lower)
            upper_sums = upper_sums + jnp.sum(upper * upper, axis=0, keepdims=True)
            lower_sums = lower_sums + jnp.sum(lower * lower, axis=0, keepdims=True)
        put_statistics(index, g, upper_sums, lower_sums)

    def fetch_loaded(i, rows):
        loads[2 * i].wait()
        loads[2 * i + 1].wait()
        return loaded[0, rows, :], loaded[1, rows, :]

    statistics(0, [piece(i, LOADS) for i in range(LOADS)], fetch_loaded)
    copy = start(
        remote(gram_out.at[0, 1 - core], gram_in.at[0], gram_send.at[0], gram_recv.at[0], partner, col)
    )

    for s in range(n_line - 2):

        @pl.when(jnp.logical_and(has_next, place > s))
        def _():
            pl.semaphore_signal(up_sem.at[s], inc=1, device_id={"row": row + 2, "col": col}, device_id_type=MESH)

        @pl.when(jnp.logical_and(has_prev, place < n_line - 1 - s))
        def _():
            pl.semaphore_signal(down_sem.at[s], inc=1, device_id={"row": row - 2, "col": col}, device_id_type=MESH)

        @pl.when(place > s + 1)
        def _():
            pl.semaphore_wait(up_sem.at[s], 1)

        @pl.when(place < n_line - 2 - s)
        def _():
            pl.semaphore_wait(down_sem.at[s], 1)

    copy.wait_recv()
    own_copy = share(0, reduce_line(gram_out[0, core] + gram_in[0]))
    for k in range(2):
        start(
            remote(
                totals.at[0, core], others.at[core], other_send.at[k], other_recv.at[core],
                chip_row + k, shift_to,
            )
        )
    for k in range(2):
        start(
            remote(
                totals.at[0, core], besides.at[core], beside_send.at[k], beside_recv.at[core],
                chip_row + k, beside,
            )
        )
    own_copy.wait_recv()
    p = coupling(totals[0, :, :half, :], totals[0, 0, half:, :])
    upper, lower = loaded[0], loaded[1]
    d = upper - tall_dot(lower, wide(p.T))
    x_wide, p_wide = wide(2.0 * inverse(p)), wide(p)
    upper_slot, lower_slot = 2 - 2 * even, 1 + even

    def place_turned(rows, size):
        new_upper, new_lower = turn(
            loaded[0, rows, :], loaded[1, rows, :], x_wide, p_wide, d[rows.start : rows.start + size]
        )
        home[upper_slot, rows, :] = new_upper
        home[lower_slot, rows, :] = new_lower

    def eighths(first, last):
        return pl.ds(first * (depth // 8), (last - first) * (depth // 8))

    move_rows = [eighths(0, RAW_FROM), eighths(0, RECEIVED_FIRST), eighths(RECEIVED_FIRST, RELAYED)]

    def move_copy(i, slot):
        return remote(
            home.at[slot, move_rows[i]], work.at[slot, move_rows[i]],
            move_send.at[i], move_recv.at[i], row, beside,
        )

    shifts = []
    shift_rows = [piece(i, SHIFTS, early) for i in range(SHIFTS)]
    for i, rows in enumerate(shift_rows):
        place_turned(rows, rows.size)
        shifts.append(
            start(
                remote(
                    home.at[2, rows], home.at[even, rows], shift_send.at[i], shift_recv.at[i],
                    row, shift_to,
                )
            )
        )
    place_turned(early_rows, early)
    start(move_copy(0, odd))
    for k in range(2):
        remote(
            totals.at[0, k], others.at[k], other_send.at[k], other_recv.at[k], row, shift_to
        ).wait_recv()
    p = coupling(others[:, :half, :], others[0, half:, :])
    for copy in relays:
        copy.wait_recv()
    upper, lower = relayed[0], relayed[1]
    d = upper - tall_dot(lower, wide(p.T))
    new_upper, new_lower = turn(upper, lower, wide(2.0 * inverse(p)), wide(p), d)
    home[2 * even, early_rows, :] = new_upper
    home[2 - even, early_rows, :] = new_lower

    start(move_copy(1, even))

    def fetch_shifted(i, rows):
        if i > 0:
            shifts[i - 1].wait_recv()
        return home[0, rows, :], home[1, rows, :]

    statistics(1, [early_rows] + shift_rows, fetch_shifted)
    copy = start(
        remote(gram_out.at[1, 1 - core], gram_in.at[1], gram_send.at[1], gram_recv.at[1], partner, col)
    )
    for k in range(2):
        remote(
            totals.at[0, k], besides.at[k], beside_send.at[k], beside_recv.at[k], row, beside
        ).wait_recv()
    p = coupling(besides[:, :half, :], besides[0, half:, :])
    back, p_wide, state = wide(p.T), wide(p), inverse_first(p, MIDDLE)
    copy.wait_recv()
    line_out[1] = gram_out[1, core] + gram_in[1]
    crossing = [
        start(
            remote(
                line_out.at[1], cross_in.at[k], cross_send.at[k], cross_recv.at[k], line_row(k), beside
            )
        )
        for k in reversed(range(n_line))
    ]
    start(move_copy(2, even))
    x_wide = wide(2.0 * inverse_last(state, MIDDLE))
    for copy in swaps:
        copy.wait_recv()

    def place_swapped(rows):
        upper, lower = swapped[0, rows, :], swapped[1, rows, :]
        new_upper, new_lower = turn(upper, lower, x_wide, p_wide, upper - tall_dot(lower, back))
        work[2 - 2 * odd, rows, :] = new_upper
        work[1 + odd, rows, :] = new_lower

    late_rows = eighths(RELAYED, 8)
    place_swapped(late_rows)
    carried = start(
        remote(
            work.at[2, late_rows], work.at[odd, late_rows], carry_send.at[0], carry_recv.at[0], row, carry_to
        )
    )
    place_swapped(eighths(RAW_FROM, RELAYED))
    total = 0.0
    for k in range(n_line):
        crossing[n_line - 1 - k].wait_recv()
        total = total + cross_in[k]
    share(1, total).wait_recv()
    out_p[...] = coupling(totals[1, :, :half, :], totals[1, 0, half:, :])
    carried.wait_recv()
    for i, slot in enumerate((even, odd, odd)):
        move_copy(i, slot).wait_recv()
    for copy in pending:
        copy.wait_send()


def finish(work, p_ref, out_upper, out_lower, stage, sems):
    depth, width = out_upper.shape
    chunk = depth // STORES
    p = p_ref[...]
    d = work[0] - tall_dot(work[1], wide(p.T))
    p_wide, x_wide = wide(p), wide(2.0 * inverse_adaptive(p))
    copies = []
    for i in range(STORES):
        rows = pl.ds(i * chunk, chunk)
        y = turn(work[0, rows, :], work[1, rows, :], x_wide, p_wide, d[i * chunk : (i + 1) * chunk])
        for which, out in enumerate((out_upper, out_lower)):
            stage[which, rows, :] = y[which]
            copies.append(pltpu.make_async_copy(stage.at[which, rows], out.at[rows], sems.at[which, i]))
            copies[-1].start()
    for copy in copies:
        copy.wait()


def shards(n_row, n_col, upper_blocks, lower_blocks):
    depth, width = upper_blocks.shape
    half = width // 2
    n_line = n_row // 2
    out = jax.ShapeDtypeStruct((depth, width), F32)
    dma = pltpu.SemaphoreType.DMA
    flag = pltpu.SemaphoreType.REGULAR
    work, p = pl.pallas_call(
        functools.partial(kernel, n_row, n_col),
        out_shape=(pltpu.VMEM((3, depth, width), F32), pltpu.VMEM((width, width), F32)),
        in_specs=[pl.BlockSpec(memory_space=pl.ANY)] * 2,
        out_specs=(pl.BlockSpec(memory_space=pltpu.VMEM),) * 2,
        scratch_shapes=[
            pltpu.VMEM((2, depth, width), F32),
            pltpu.VMEM((2, RELAYED * (depth // 8), width), F32),
            pltpu.VMEM((2, depth, width), F32),
            pltpu.VMEM((3, depth, width), F32),
            pltpu.VMEM((ROUNDS, 2, half + 8, width), F32),
            pltpu.VMEM((2, half + 8, width), F32),
            pltpu.VMEM((ROUNDS, half + 8, width), F32),
            pltpu.VMEM((n_line - 1, half + 8, width), F32),
            pltpu.VMEM((n_line, half + 8, width), F32),
            pltpu.VMEM((ROUNDS, 2, half + 8, width), F32),
            pltpu.VMEM((2, half + 8, width), F32),
            pltpu.VMEM((2, half + 8, width), F32),
            dma((2,)),
            dma((2,)),
            dma((n_line - 1,)),
            dma((n_line - 1,)),
            dma((n_line,)),
            dma((n_line,)),
            dma((ROUNDS,)),
            dma((ROUNDS,)),
            dma((2,)),
            dma((2,)),
            dma((2,)),
            dma((2,)),
            dma((2, 2)),
            dma((2, 2)),
            dma((2, 2)),
            dma((2, 2)),
            dma((SHIFTS,)),
            dma((SHIFTS,)),
            dma((1,)),
            dma((1,)),
            dma((3,)),
            dma((3,)),
            dma((2, LOADS)),
            flag((max(n_line - 2, 1),)),
            flag((max(n_line - 2, 1),)),
        ],
        compiler_params=pltpu.CompilerParams(collective_id=0, has_side_effects=True),
    )(upper_blocks, lower_blocks)
    return pl.pallas_call(
        finish,
        out_shape=(out, out),
        in_specs=[pl.BlockSpec(memory_space=pltpu.VMEM)] * 2,
        out_specs=(pl.BlockSpec(memory_space=pl.ANY),) * 2,
        scratch_shapes=[pltpu.VMEM((2, depth, width), F32), dma((2, STORES))],
    )(*(pltpu.with_memory_space_constraint(x, pltpu.VMEM) for x in (work, p)))


def solution(mesh):
    placed = (P("row", "col"), P("row", "col"))
    return jax.shard_map(
        functools.partial(shards, mesh.shape["row"], mesh.shape["col"]),
        mesh=mesh,
        in_specs=placed,
        out_specs=(P("row", "col"), P("row", "col")),
        check_vma=False,
    )
```

```python
import functools

import jax
import jax.numpy as jnp
from jax import lax
from jax.experimental import pallas as pl
from jax.experimental.pallas import tpu as pltpu
from jax.sharding import PartitionSpec as P

ROUNDS = 2
LOADS = 2
RELAYED = 5
RAW_FROM = 2
RECEIVED_FIRST = 3
SHIFTS = 1
EXACT_ABOVE = 1.0
STORES = 4
MESH = pl.DeviceIdType.MESH
F32 = jnp.float32
BF16 = jnp.bfloat16


def split(x):
    high = x.astype(BF16)
    low = (x - high.astype(F32)).astype(BF16)
    return high, low


def split_three(x):
    high = x.astype(BF16)
    rest = x - high.astype(F32)
    middle = rest.astype(BF16)
    return high, middle, (rest - middle.astype(F32)).astype(BF16)


def fast_dot(a, b):
    return jnp.dot(a, b, preferred_element_type=F32)


def exact_dot(a, b):
    width = b.shape[1]
    (a0, a1, a2), (b0, b1, b2) = split_three(a), split_three(b)
    upper = jnp.concatenate([b0, b1], axis=1)
    lower = jnp.concatenate([b1, b0], axis=1)
    large = fast_dot(jnp.concatenate([a0, a1], axis=1), jnp.concatenate([upper, lower], axis=0))
    small = fast_dot(jnp.concatenate([a0, a2], axis=1), jnp.concatenate([b2, b0], axis=0))
    return large[:, :width] + (large[:, width:] + small)


def wide(b):
    both = jnp.concatenate(split(b), axis=1)
    return jnp.concatenate([both, both], axis=0)


def tall_dot(a, b_wide):
    width = a.shape[1]
    y = fast_dot(jnp.concatenate(split(a), axis=1), b_wide)
    return y[:, :width] + y[:, width:]


def gram(upper, lower):
    width = upper.shape[1]
    left = jnp.concatenate(split(upper), axis=1)
    right = jnp.concatenate(split(lower), axis=1)
    q = lax.dot_general(
        left, right, (((0,), (0,)), ((), ())), preferred_element_type=F32
    )
    return q[:width, :width] + (q[:width, width:] + q[width:, :width])


def identity(width):
    rows = lax.broadcasted_iota(jnp.int32, (width, width), 0)
    lanes = lax.broadcasted_iota(jnp.int32, (width, width), 1)
    return (rows == lanes).astype(F32)


def shrink(spread):
    square = spread * spread
    gain = 2.0 / (2.0 - square)
    return gain, 0.5 * square * gain


def step_count(width):
    square = (width / 4.0) ** 2
    spread = 0.5 * square / (1.0 + 0.5 * square)
    steps = 0
    while spread > 1e-3:
        spread = shrink(spread)[1]
        steps += 1
    return steps


def quick_dot(a, b):
    return tall_dot(a, wide(b))


def correct(s, x):
    e = (identity(x.shape[0]) - x) - exact_dot(s, x)
    return x + quick_dot(x, e)


def inverse(p):
    width = p.shape[0]
    eye = identity(width)
    s = exact_dot(p, p.T)
    total = jnp.sum(jnp.sum(p * p, axis=0, keepdims=True), axis=1, keepdims=True)
    total = jnp.broadcast_to(total, (1, width))
    scale = 1.0 / (1.0 + 0.5 * total)
    spread = 0.5 * total * scale
    e = spread * eye - scale * s
    x = None
    steps = step_count(width)
    for step in range(steps):
        gain, spread = shrink(spread)
        if step == 0:
            x = (gain * scale) * (eye + e)
        else:
            x = gain * (x + quick_dot(x, e))
        if step < steps - 1:
            e = gain * quick_dot(e, e) - spread * eye
    return correct(s, x)


def inverse_adaptive(p):
    width = p.shape[0]
    eye = identity(width)
    s = exact_dot(p, p.T)
    bound = 1.0001 * jnp.max(jnp.sum(jnp.abs(s), axis=0, keepdims=True))
    scale = 1.0 / (1.0 + 0.5 * bound)
    spread = 0.5 * bound * scale
    e = spread * eye - scale * s
    gain, spread = shrink(spread)
    x = (gain * scale) * (eye + e)
    squared = exact_dot(e, e)

    def body(state):
        x, squared, gain, spread = state
        e = gain * squared - spread * eye
        gain, spread = shrink(spread)
        return gain * (x + exact_dot(x, e)), exact_dot(e, e), gain, spread

    x = lax.while_loop(lambda state: state[3] > 3e-6, body, (x, squared, gain, spread))[0]
    return lax.cond(bound > EXACT_ABOVE, lambda: correct(s, x), lambda: x)


def turn(upper, lower, x_wide, p_wide, d):
    v = tall_dot(d, x_wide)
    return v - upper, lower + tall_dot(v, p_wide)


def kernel(
    n_row, n_col, upper_hbm, lower_hbm, work, out_p,
    loaded, relayed, swapped, home, gram_out, gram_in, line_out, line_in, cross_in, totals, others, besides,
    gram_send, gram_recv, line_send, line_recv, cross_send, cross_recv,
    pair_send, pair_recv, other_send, other_recv, beside_send, beside_recv,
    relay_send, relay_recv, swap_send, swap_recv, shift_send, shift_recv, carry_send, carry_recv, move_send, move_recv, load_sem, up_sem, down_sem,
):
    depth, width = upper_hbm.shape
    half = width // 2
    n_line = n_row // 2
    row_total = float(depth * n_row)
    row, col = lax.axis_index("row"), lax.axis_index("col")
    core = lax.rem(row, 2)
    chip_row = row - core
    place = chip_row // 2
    partner = chip_row + 1 - core
    odd = lax.rem(col, 2)
    even = 1 - odd
    beside = col + 1 - 2 * odd
    ahead = lax.rem(col + 2, n_col)
    behind = lax.rem(col + n_col - 2, n_col)
    shift_to = ahead + even * (behind - ahead)
    carry_to = ahead + odd * (behind - ahead)
    has_prev, has_next = place > 0, place < n_line - 1
    early = RELAYED * (depth // 8)
    early_rows = pl.ds(0, early)

    def line_row(k):
        return lax.rem(row + 2 * k, n_row)

    def piece(i, count, first=0, last=None):
        size = ((depth if last is None else last) - first) // count
        return pl.ds(first + i * size, size)

    loads = []
    for i in range(LOADS):
        rows = piece(i, LOADS)
        for which, ref in enumerate((upper_hbm, lower_hbm)):
            loads.append(pltpu.make_async_copy(ref.at[rows], loaded.at[which, rows], load_sem.at[which, i]))
            loads[-1].start()
    barrier = pltpu.get_barrier_semaphore()

    def greet(r, c):
        pl.semaphore_signal(barrier, inc=1, device_id={"row": r, "col": c}, device_id_type=MESH)

    greeted = [(chip_row, beside), (chip_row + 1, beside), (partner, col)]
    for c in [ahead] + ([] if n_col == 4 else [behind]):
        greeted += [(chip_row, c), (chip_row + 1, c)]
    for r, c in greeted:
        greet(r, c)

    @pl.when(has_prev)
    def _():
        greet(row - 2, col)

    @pl.when(has_next)
    def _():
        greet(row + 2, col)

    pl.semaphore_wait(barrier, len(greeted) + has_prev.astype(jnp.int32) + has_next.astype(jnp.int32))

    def remote(src, dst, send, recv, r, c):
        return pltpu.make_async_remote_copy(
            src_ref=src, dst_ref=dst, send_sem=send, recv_sem=recv,
            device_id={"row": r, "col": c}, device_id_type=MESH,
        )

    pending = []

    def start(copy):
        copy.start()
        pending.append(copy)
        return copy

    def send_raw(i, first, last, dst, send, recv, c):
        rows = pl.ds(first * (depth // 8), (last - first) * (depth // 8))
        return [
            start(remote(ref.at[rows], dst.at[which, rows], send.at[which, i], recv.at[which, i], row, c))
            for which, ref in enumerate((upper_hbm, lower_hbm))
        ]

    def relay(i, first, last):
        return send_raw(i, first, last, relayed, relay_send, relay_recv, shift_to)

    def swap(i, first, last):
        return send_raw(i, first, last, swapped, swap_send, swap_recv, beside)

    relays = relay(0, 0, RELAYED)
    swaps = swap(0, RAW_FROM, 8)

    def put_statistics(index, g, upper_sums, lower_sums):
        which = lax.broadcasted_iota(jnp.int32, (8, width), 0)
        norms = jnp.where(which == 0, upper_sums, jnp.where(which == 1, lower_sums, 0.0))
        for k in range(2):
            gram_out[index, k, :half, :] = g[k * half : (k + 1) * half]
            gram_out[index, k, half:, :] = norms

    def share(index, total):
        totals[index, core] = total
        return start(
            remote(
                totals.at[index, core], totals.at[index, core],
                pair_send.at[index], pair_recv.at[index], partner, col,
            )
        )

    def reduce_line(own):
        line_out[0] = own
        copies = []
        for k in range(1, n_line):
            copies.append(
                start(
                    remote(
                        line_out.at[0], line_in.at[k - 1],
                        line_send.at[k - 1], line_recv.at[k - 1], line_row(k), col,
                    )
                )
            )
        total = own
        for k in range(1, n_line):
            copies[k - 1].wait_recv()
            total = total + line_in[k - 1]
        return total

    def coupling(both_halves, norm_rows):
        norms = norm_rows / row_total
        a_row, b = norms[:1], norms[1:2]
        a = jnp.broadcast_to(a_row, (width, width)).T
        gap, both = a - b, a + b
        factor = -gap / (2.0 * gap * gap + 0.5 * both * both + 1e-05)
        return (both_halves.reshape(width, width) / row_total) * factor

    def statistics(index, pieces, fetch):
        g, upper_sums, lower_sums = 0.0, 0.0, 0.0
        for i, rows in enumerate(pieces):
            upper, lower = fetch(i, rows)
            g = g + gram(upper, lower)
            upper_sums = upper_sums + jnp.sum(upper * upper, axis=0, keepdims=True)
            lower_sums = lower_sums + jnp.sum(lower * lower, axis=0, keepdims=True)
        put_statistics(index, g, upper_sums, lower_sums)

    def fetch_loaded(i, rows):
        loads[2 * i].wait()
        loads[2 * i + 1].wait()
        return loaded[0, rows, :], loaded[1, rows, :]

    statistics(0, [piece(i, LOADS) for i in range(LOADS)], fetch_loaded)
    copy = start(
        remote(gram_out.at[0, 1 - core], gram_in.at[0], gram_send.at[0], gram_recv.at[0], partner, col)
    )

    for s in range(n_line - 2):

        @pl.when(jnp.logical_and(has_next, place > s))
        def _():
            pl.semaphore_signal(up_sem.at[s], inc=1, device_id={"row": row + 2, "col": col}, device_id_type=MESH)

        @pl.when(jnp.logical_and(has_prev, place < n_line - 1 - s))
        def _():
            pl.semaphore_signal(down_sem.at[s], inc=1, device_id={"row": row - 2, "col": col}, device_id_type=MESH)

        @pl.when(place > s + 1)
        def _():
            pl.semaphore_wait(up_sem.at[s], 1)

        @pl.when(place < n_line - 2 - s)
        def _():
            pl.semaphore_wait(down_sem.at[s], 1)

    copy.wait_recv()
    own_copy = share(0, reduce_line(gram_out[0, core] + gram_in[0]))
    for k in range(2):
        start(
            remote(
                totals.at[0, core], others.at[core], other_send.at[k], other_recv.at[core],
                chip_row + k, shift_to,
            )
        )
    for k in range(2):
        start(
            remote(
                totals.at[0, core], besides.at[core], beside_send.at[k], beside_recv.at[core],
                chip_row + k, beside,
            )
        )
    own_copy.wait_recv()
    p = coupling(totals[0, :, :half, :], totals[0, 0, half:, :])
    upper, lower = loaded[0], loaded[1]
    d = upper - tall_dot(lower, wide(p.T))
    x_wide, p_wide = wide(2.0 * inverse(p)), wide(p)
    upper_slot, lower_slot = 2 - 2 * even, 1 + even

    def place_turned(rows, size):
        new_upper, new_lower = turn(
            loaded[0, rows, :], loaded[1, rows, :], x_wide, p_wide, d[rows.start : rows.start + size]
        )
        home[upper_slot, rows, :] = new_upper
        home[lower_slot, rows, :] = new_lower

    def eighths(first, last):
        return pl.ds(first * (depth // 8), (last - first) * (depth // 8))

    move_rows = [eighths(0, RAW_FROM), eighths(0, RECEIVED_FIRST), eighths(RECEIVED_FIRST, RELAYED)]

    def move_copy(i, slot):
        return remote(
            home.at[slot, move_rows[i]], work.at[slot, move_rows[i]],
            move_send.at[i], move_recv.at[i], row, beside,
        )

    shifts = []
    shift_rows = [piece(i, SHIFTS, early) for i in range(SHIFTS)]
    for i, rows in enumerate(shift_rows):
        place_turned(rows, rows.size)
        shifts.append(
            start(
                remote(
                    home.at[2, rows], home.at[even, rows], shift_send.at[i], shift_recv.at[i],
                    row, shift_to,
                )
            )
        )
    place_turned(early_rows, early)
    start(move_copy(0, odd))
    for k in range(2):
        remote(
            totals.at[0, k], others.at[k], other_send.at[k], other_recv.at[k], row, shift_to
        ).wait_recv()
    p = coupling(others[:, :half, :], others[0, half:, :])
    for copy in relays:
        copy.wait_recv()
    upper, lower = relayed[0], relayed[1]
    d = upper - tall_dot(lower, wide(p.T))
    new_upper, new_lower = turn(upper, lower, wide(2.0 * inverse(p)), wide(p), d)
    home[2 * even, early_rows, :] = new_upper
    home[2 - even, early_rows, :] = new_lower

    start(move_copy(1, even))

    def fetch_shifted(i, rows):
        if i > 0:
            shifts[i - 1].wait_recv()
        return home[0, rows, :], home[1, rows, :]

    statistics(1, [early_rows] + shift_rows, fetch_shifted)
    copy = start(
        remote(gram_out.at[1, 1 - core], gram_in.at[1], gram_send.at[1], gram_recv.at[1], partner, col)
    )
    copy.wait_recv()
    line_out[1] = gram_out[1, core] + gram_in[1]
    crossing = [
        start(
            remote(
                line_out.at[1], cross_in.at[k], cross_send.at[k], cross_recv.at[k], line_row(k), beside
            )
        )
        for k in reversed(range(n_line))
    ]
    start(move_copy(2, even))
    for k in range(2):
        remote(
            totals.at[0, k], besides.at[k], beside_send.at[k], beside_recv.at[k], row, beside
        ).wait_recv()
    p = coupling(besides[:, :half, :], besides[0, half:, :])
    back, p_wide, x_wide = wide(p.T), wide(p), wide(2.0 * inverse(p))
    for copy in swaps:
        copy.wait_recv()

    def place_swapped(rows):
        upper, lower = swapped[0, rows, :], swapped[1, rows, :]
        new_upper, new_lower = turn(upper, lower, x_wide, p_wide, upper - tall_dot(lower, back))
        work[2 - 2 * odd, rows, :] = new_upper
        work[1 + odd, rows, :] = new_lower

    late_rows = eighths(RELAYED, 8)
    place_swapped(late_rows)
    carried = start(
        remote(
            work.at[2, late_rows], work.at[odd, late_rows], carry_send.at[0], carry_recv.at[0], row, carry_to
        )
    )
    place_swapped(eighths(RAW_FROM, RELAYED))
    total = 0.0
    for k in range(n_line):
        crossing[n_line - 1 - k].wait_recv()
        total = total + cross_in[k]
    share(1, total).wait_recv()
    out_p[...] = coupling(totals[1, :, :half, :], totals[1, 0, half:, :])
    carried.wait_recv()
    for i, slot in enumerate((even, odd, odd)):
        move_copy(i, slot).wait_recv()
    for copy in pending:
        copy.wait_send()


def finish(work, p_ref, out_upper, out_lower, stage, sems):
    depth, width = out_upper.shape
    chunk = depth // STORES
    p = p_ref[...]
    d = work[0] - tall_dot(work[1], wide(p.T))
    p_wide, x_wide = wide(p), wide(2.0 * inverse_adaptive(p))
    copies = []
    for i in range(STORES):
        rows = pl.ds(i * chunk, chunk)
        y = turn(work[0, rows, :], work[1, rows, :], x_wide, p_wide, d[i * chunk : (i + 1) * chunk])
        for which, out in enumerate((out_upper, out_lower)):
            stage[which, rows, :] = y[which]
            copies.append(pltpu.make_async_copy(stage.at[which, rows], out.at[rows], sems.at[which, i]))
            copies[-1].start()
    for copy in copies:
        copy.wait()


def shards(n_row, n_col, upper_blocks, lower_blocks):
    depth, width = upper_blocks.shape
    half = width // 2
    n_line = n_row // 2
    out = jax.ShapeDtypeStruct((depth, width), F32)
    dma = pltpu.SemaphoreType.DMA
    flag = pltpu.SemaphoreType.REGULAR
    work, p = pl.pallas_call(
        functools.partial(kernel, n_row, n_col),
        out_shape=(pltpu.VMEM((3, depth, width), F32), pltpu.VMEM((width, width), F32)),
        in_specs=[pl.BlockSpec(memory_space=pl.ANY)] * 2,
        out_specs=(pl.BlockSpec(memory_space=pltpu.VMEM),) * 2,
        scratch_shapes=[
            pltpu.VMEM((2, depth, width), F32),
            pltpu.VMEM((2, RELAYED * (depth // 8), width), F32),
            pltpu.VMEM((2, depth, width), F32),
            pltpu.VMEM((3, depth, width), F32),
            pltpu.VMEM((ROUNDS, 2, half + 8, width), F32),
            pltpu.VMEM((2, half + 8, width), F32),
            pltpu.VMEM((ROUNDS, half + 8, width), F32),
            pltpu.VMEM((n_line - 1, half + 8, width), F32),
            pltpu.VMEM((n_line, half + 8, width), F32),
            pltpu.VMEM((ROUNDS, 2, half + 8, width), F32),
            pltpu.VMEM((2, half + 8, width), F32),
            pltpu.VMEM((2, half + 8, width), F32),
            dma((2,)),
            dma((2,)),
            dma((n_line - 1,)),
            dma((n_line - 1,)),
            dma((n_line,)),
            dma((n_line,)),
            dma((ROUNDS,)),
            dma((ROUNDS,)),
            dma((2,)),
            dma((2,)),
            dma((2,)),
            dma((2,)),
            dma((2, 2)),
            dma((2, 2)),
            dma((2, 2)),
            dma((2, 2)),
            dma((SHIFTS,)),
            dma((SHIFTS,)),
            dma((1,)),
            dma((1,)),
            dma((3,)),
            dma((3,)),
            dma((2, LOADS)),
            flag((max(n_line - 2, 1),)),
            flag((max(n_line - 2, 1),)),
        ],
        compiler_params=pltpu.CompilerParams(collective_id=0, has_side_effects=True),
    )(upper_blocks, lower_blocks)
    return pl.pallas_call(
        finish,
        out_shape=(out, out),
        in_specs=[pl.BlockSpec(memory_space=pltpu.VMEM)] * 2,
        out_specs=(pl.BlockSpec(memory_space=pl.ANY),) * 2,
        scratch_shapes=[pltpu.VMEM((2, depth, width), F32), dma((2, STORES))],
    )(*(pltpu.with_memory_space_constraint(x, pltpu.VMEM) for x in (work, p)))


def solution(mesh):
    placed = (P("row", "col"), P("row", "col"))
    return jax.shard_map(
        functools.partial(shards, mesh.shape["row"], mesh.shape["col"]),
        mesh=mesh,
        in_specs=placed,
        out_specs=(P("row", "col"), P("row", "col")),
        check_vma=False,
    )
```

```python
import functools

import jax
import jax.numpy as jnp
from jax import lax
from jax.experimental import pallas as pl
from jax.experimental.pallas import tpu as pltpu
from jax.sharding import PartitionSpec as P

ROUNDS = 2
LOADS = 1
RELAYED = 5
RELAYED_FIRST = 5
RAW_FROM = 2
RECEIVED_FIRST = 3
SHIFTS = 1
EXACT_ABOVE = 1.0
STORES = 4
MESH = pl.DeviceIdType.MESH
F32 = jnp.float32
BF16 = jnp.bfloat16


def split(x):
    high = x.astype(BF16)
    low = (x - high.astype(F32)).astype(BF16)
    return high, low


def split_three(x):
    high = x.astype(BF16)
    rest = x - high.astype(F32)
    middle = rest.astype(BF16)
    return high, middle, (rest - middle.astype(F32)).astype(BF16)


def fast_dot(a, b):
    return jnp.dot(a, b, preferred_element_type=F32)


def exact_dot(a, b):
    width = b.shape[1]
    (a0, a1, a2), (b0, b1, b2) = split_three(a), split_three(b)
    upper = jnp.concatenate([b0, b1], axis=1)
    lower = jnp.concatenate([b1, b0], axis=1)
    large = fast_dot(jnp.concatenate([a0, a1], axis=1), jnp.concatenate([upper, lower], axis=0))
    small = fast_dot(jnp.concatenate([a0, a2], axis=1), jnp.concatenate([b2, b0], axis=0))
    return large[:, :width] + (large[:, width:] + small)


def wide(b):
    both = jnp.concatenate(split(b), axis=1)
    return jnp.concatenate([both, both], axis=0)


def tall_dot(a, b_wide):
    width = a.shape[1]
    y = fast_dot(jnp.concatenate(split(a), axis=1), b_wide)
    return y[:, :width] + y[:, width:]


def gram(upper, lower):
    width = upper.shape[1]
    left = jnp.concatenate(split(upper), axis=1)
    right = jnp.concatenate(split(lower), axis=1)
    q = lax.dot_general(
        left, right, (((0,), (0,)), ((), ())), preferred_element_type=F32
    )
    return q[:width, :width] + (q[:width, width:] + q[width:, :width])


def identity(width):
    rows = lax.broadcasted_iota(jnp.int32, (width, width), 0)
    lanes = lax.broadcasted_iota(jnp.int32, (width, width), 1)
    return (rows == lanes).astype(F32)


def shrink(spread):
    square = spread * spread
    gain = 2.0 / (2.0 - square)
    return gain, 0.5 * square * gain


def step_count(width):
    square = (width / 4.0) ** 2
    spread = 0.5 * square / (1.0 + 0.5 * square)
    steps = 0
    while spread > 1e-3:
        spread = shrink(spread)[1]
        steps += 1
    return steps


def quick_dot(a, b):
    return tall_dot(a, wide(b))


def correct(s, x):
    e = (identity(x.shape[0]) - x) - exact_dot(s, x)
    return x + quick_dot(x, e)


def inverse(p):
    width = p.shape[0]
    eye = identity(width)
    s = exact_dot(p, p.T)
    total = jnp.sum(jnp.sum(p * p, axis=0, keepdims=True), axis=1, keepdims=True)
    total = jnp.broadcast_to(total, (1, width))
    scale = 1.0 / (1.0 + 0.5 * total)
    spread = 0.5 * total * scale
    e = spread * eye - scale * s
    x = None
    steps = step_count(width)
    for step in range(steps):
        gain, spread = shrink(spread)
        if step == 0:
            x = (gain * scale) * (eye + e)
        else:
            x = gain * (x + quick_dot(x, e))
        if step < steps - 1:
            e = gain * quick_dot(e, e) - spread * eye
    return correct(s, x)


def inverse_adaptive(p):
    width = p.shape[0]
    eye = identity(width)
    s = exact_dot(p, p.T)
    bound = 1.0001 * jnp.max(jnp.sum(jnp.abs(s), axis=0, keepdims=True))
    scale = 1.0 / (1.0 + 0.5 * bound)
    spread = 0.5 * bound * scale
    squared = (scale * scale) * exact_dot(s, s) + (spread * spread) * eye - (2.0 * spread * scale) * s
    gain, smaller = shrink(spread)
    x = (gain * scale) * ((1.0 + spread) * eye - scale * s)

    def body(state):
        x, e, spread = state
        gain, spread = shrink(spread)
        return gain * (x + quick_dot(x, e)), gain * quick_dot(e, e) - spread * eye, spread

    x = lax.while_loop(lambda state: state[2] > 3e-6, body, (x, gain * squared - smaller * eye, smaller))[0]
    return lax.cond(bound > EXACT_ABOVE, lambda: correct(s, x), lambda: x)


def turn(upper, lower, x_wide, p_wide, d):
    v = tall_dot(d, x_wide)
    return v - upper, lower + tall_dot(v, p_wide)


def kernel(
    n_row, n_col, upper_hbm, lower_hbm, work, out_p,
    loaded, relayed, swapped, home, gram_out, gram_in, line_out, line_in, cross_in, totals, others, besides,
    gram_send, gram_recv, line_send, line_recv, cross_send, cross_recv,
    pair_send, pair_recv, other_send, other_recv, beside_send, beside_recv,
    relay_send, relay_recv, swap_send, swap_recv, shift_send, shift_recv, carry_send, carry_recv, move_send, move_recv, load_sem, up_sem, down_sem,
):
    depth, width = upper_hbm.shape
    half = width // 2
    n_line = n_row // 2
    row_total = float(depth * n_row)
    row, col = lax.axis_index("row"), lax.axis_index("col")
    core = lax.rem(row, 2)
    chip_row = row - core
    place = chip_row // 2
    partner = chip_row + 1 - core
    odd = lax.rem(col, 2)
    even = 1 - odd
    beside = col + 1 - 2 * odd
    ahead = lax.rem(col + 2, n_col)
    behind = lax.rem(col + n_col - 2, n_col)
    shift_to = ahead + even * (behind - ahead)
    carry_to = ahead + odd * (behind - ahead)
    has_prev, has_next = place > 0, place < n_line - 1
    early = RELAYED * (depth // 8)
    early_rows = pl.ds(0, early)
    line = pl.ds(0, half + 1)

    def line_row(k):
        return lax.rem(row + 2 * k, n_row)

    def piece(i, count, first=0, last=None):
        size = ((depth if last is None else last) - first) // count
        return pl.ds(first + i * size, size)

    loads = []
    for i in range(LOADS):
        rows = piece(i, LOADS)
        for which, ref in enumerate((upper_hbm, lower_hbm)):
            loads.append(pltpu.make_async_copy(ref.at[rows], loaded.at[which, rows], load_sem.at[which, i]))
            loads[-1].start()
    barrier = pltpu.get_barrier_semaphore()

    def greet(r, c):
        pl.semaphore_signal(barrier, inc=1, device_id={"row": r, "col": c}, device_id_type=MESH)

    greeted = [(chip_row, beside), (chip_row + 1, beside), (partner, col)]
    for c in [ahead] + ([] if n_col == 4 else [behind]):
        greeted += [(chip_row, c), (chip_row + 1, c)]
    for r, c in greeted:
        greet(r, c)

    @pl.when(has_prev)
    def _():
        greet(row - 2, col)

    @pl.when(has_next)
    def _():
        greet(row + 2, col)

    pl.semaphore_wait(barrier, len(greeted) + has_prev.astype(jnp.int32) + has_next.astype(jnp.int32))

    def remote(src, dst, send, recv, r, c):
        return pltpu.make_async_remote_copy(
            src_ref=src, dst_ref=dst, send_sem=send, recv_sem=recv,
            device_id={"row": r, "col": c}, device_id_type=MESH,
        )

    pending = []

    def start(copy):
        copy.start()
        pending.append(copy)
        return copy

    def send_raw(i, first, last, dst, send, recv, c):
        rows = pl.ds(first * (depth // 8), (last - first) * (depth // 8))
        return [
            start(remote(ref.at[rows], dst.at[which, rows], send.at[which, i], recv.at[which, i], row, c))
            for which, ref in enumerate((upper_hbm, lower_hbm))
        ]

    def relay(i, first, last):
        return send_raw(i, first, last, relayed, relay_send, relay_recv, shift_to)

    def swap(i, first, last):
        return send_raw(i, first, last, swapped, swap_send, swap_recv, beside)

    relays = relay(0, 0, RELAYED_FIRST)
    swaps = swap(0, RAW_FROM, 8)

    def put_statistics(index, g, upper_sums, lower_sums):
        for k, sums in enumerate((upper_sums, lower_sums)):
            gram_out[index, k, :half, :] = g[k * half : (k + 1) * half]
            gram_out[index, k, half : half + 1, :] = sums

    def share(index, total):
        totals[index, core, line, :] = total
        return start(
            remote(
                totals.at[index, core, line], totals.at[index, core, line],
                pair_send.at[index], pair_recv.at[index], partner, col,
            )
        )

    def reduce_line(own):
        line_out[0, line, :] = own
        copies = []
        for k in range(1, n_line):
            copies.append(
                start(
                    remote(
                        line_out.at[0, line], line_in.at[k - 1, line],
                        line_send.at[k - 1], line_recv.at[k - 1], line_row(k), col,
                    )
                )
            )
        total = own
        for k in range(1, n_line):
            copies[k - 1].wait_recv()
            total = total + line_in[k - 1, line, :]
        return total

    def coupling(read):
        both_halves = jnp.concatenate([read(k, slice(0, half)) for k in range(2)], axis=0)
        a_row, b = (read(k, slice(half, half + 1)) / row_total for k in range(2))
        a = jnp.broadcast_to(a_row, (width, width)).T
        gap, both = a - b, a + b
        factor = -gap / (2.0 * gap * gap + 0.5 * both * both + 1e-05)
        return (both_halves / row_total) * factor

    def statistics(index, pieces, fetch):
        g, upper_sums, lower_sums = 0.0, 0.0, 0.0
        for i, rows in enumerate(pieces):
            upper, lower = fetch(i, rows)
            g = g + gram(upper, lower)
            upper_sums = upper_sums + jnp.sum(upper * upper, axis=0, keepdims=True)
            lower_sums = lower_sums + jnp.sum(lower * lower, axis=0, keepdims=True)
        put_statistics(index, g, upper_sums, lower_sums)

    def fetch_loaded(i, rows):
        loads[2 * i].wait()
        loads[2 * i + 1].wait()
        return loaded[0, rows, :], loaded[1, rows, :]

    statistics(0, [piece(i, LOADS) for i in range(LOADS)], fetch_loaded)
    copy = start(
        remote(gram_out.at[0, 1 - core, line], gram_in.at[0, line], gram_send.at[0], gram_recv.at[0], partner, col)
    )

    for s in range(n_line - 2):

        @pl.when(jnp.logical_and(has_next, place > s))
        def _():
            pl.semaphore_signal(up_sem.at[s], inc=1, device_id={"row": row + 2, "col": col}, device_id_type=MESH)

        @pl.when(jnp.logical_and(has_prev, place < n_line - 1 - s))
        def _():
            pl.semaphore_signal(down_sem.at[s], inc=1, device_id={"row": row - 2, "col": col}, device_id_type=MESH)

        @pl.when(place > s + 1)
        def _():
            pl.semaphore_wait(up_sem.at[s], 1)

        @pl.when(place < n_line - 2 - s)
        def _():
            pl.semaphore_wait(down_sem.at[s], 1)

    copy.wait_recv()
    own_copy = share(0, reduce_line(gram_out[0, core, line, :] + gram_in[0, line, :]))
    for k in range(2):
        start(
            remote(
                totals.at[0, core, line], others.at[core, line], other_send.at[k], other_recv.at[core],
                chip_row + k, shift_to,
            )
        )
    for k in range(2):
        start(
            remote(
                totals.at[0, core, line], besides.at[core, line], beside_send.at[k], beside_recv.at[core],
                chip_row + k, beside,
            )
        )
    if RELAYED > RELAYED_FIRST:
        relays += relay(1, RELAYED_FIRST, RELAYED)
    own_copy.wait_recv()
    p = coupling(lambda k, rows: totals[0, k, rows, :])
    upper, lower = loaded[0], loaded[1]
    d = upper - tall_dot(lower, wide(p.T))
    x_wide, p_wide = wide(2.0 * inverse(p)), wide(p)
    upper_slot, lower_slot = 2 - 2 * even, 1 + even

    def place_turned(rows, size):
        new_upper, new_lower = turn(
            loaded[0, rows, :], loaded[1, rows, :], x_wide, p_wide, d[rows.start : rows.start + size]
        )
        home[upper_slot, rows, :] = new_upper
        home[lower_slot, rows, :] = new_lower

    def eighths(first, last):
        return pl.ds(first * (depth // 8), (last - first) * (depth // 8))

    move_rows = [eighths(0, RAW_FROM), eighths(0, RECEIVED_FIRST), eighths(RECEIVED_FIRST, RELAYED)]

    def move_copy(i, slot):
        return remote(
            home.at[slot, move_rows[i]], work.at[slot, move_rows[i]],
            move_send.at[i], move_recv.at[i], row, beside,
        )

    shifts = []
    shift_rows = [piece(i, SHIFTS, early) for i in range(SHIFTS)]
    for i, rows in enumerate(shift_rows):
        place_turned(rows, rows.size)
        shifts.append(
            start(
                remote(
                    home.at[2, rows], home.at[even, rows], shift_send.at[i], shift_recv.at[i],
                    row, shift_to,
                )
            )
        )
    place_turned(early_rows, early)
    start(move_copy(0, odd))
    for k in range(2):
        remote(
            totals.at[0, k, line], others.at[k, line], other_send.at[k], other_recv.at[k], row, shift_to
        ).wait_recv()
    p = coupling(lambda k, rows: others[k, rows, :])
    for copy in relays:
        copy.wait_recv()
    upper, lower = relayed[0], relayed[1]
    d = upper - tall_dot(lower, wide(p.T))
    new_upper, new_lower = turn(upper, lower, wide(2.0 * inverse(p)), wide(p), d)
    home[2 * even, early_rows, :] = new_upper
    home[2 - even, early_rows, :] = new_lower

    start(move_copy(1, even))

    def fetch_shifted(i, rows):
        if i > 0:
            shifts[i - 1].wait_recv()
        return home[0, rows, :], home[1, rows, :]

    statistics(1, [early_rows] + shift_rows, fetch_shifted)
    copy = start(
        remote(gram_out.at[1, 1 - core, line], gram_in.at[1, line], gram_send.at[1], gram_recv.at[1], partner, col)
    )
    copy.wait_recv()
    line_out[1, line, :] = gram_out[1, core, line, :] + gram_in[1, line, :]
    crossing = [
        start(
            remote(
                line_out.at[1, line], cross_in.at[k, line], cross_send.at[k], cross_recv.at[k], line_row(k), beside
            )
        )
        for k in reversed(range(n_line))
    ]
    start(move_copy(2, even))
    for k in range(2):
        remote(
            totals.at[0, k, line], besides.at[k, line], beside_send.at[k], beside_recv.at[k], row, beside
        ).wait_recv()
    p = coupling(lambda k, rows: besides[k, rows, :])
    back, p_wide, x_wide = wide(p.T), wide(p), wide(2.0 * inverse(p))
    for copy in swaps:
        copy.wait_recv()

    def place_swapped(rows):
        upper, lower = swapped[0, rows, :], swapped[1, rows, :]
        new_upper, new_lower = turn(upper, lower, x_wide, p_wide, upper - tall_dot(lower, back))
        work[2 - 2 * odd, rows, :] = new_upper
        work[1 + odd, rows, :] = new_lower

    late_rows = eighths(RELAYED, 8)
    place_swapped(late_rows)
    carried = start(
        remote(
            work.at[2, late_rows], work.at[odd, late_rows], carry_send.at[0], carry_recv.at[0], row, carry_to
        )
    )
    place_swapped(eighths(RAW_FROM, RELAYED))
    total = 0.0
    for k in range(n_line):
        crossing[n_line - 1 - k].wait_recv()
        total = total + cross_in[k, line, :]
    share(1, total).wait_recv()
    out_p[...] = coupling(lambda k, rows: totals[1, k, rows, :])
    carried.wait_recv()
    for i, slot in enumerate((even, odd, odd)):
        move_copy(i, slot).wait_recv()
    for copy in pending:
        copy.wait_send()


def finish(work, p_ref, out_upper, out_lower, stage, sems):
    depth, width = out_upper.shape
    chunk = depth // STORES
    p = p_ref[...]
    d = work[0] - tall_dot(work[1], wide(p.T))
    p_wide, x_wide = wide(p), wide(2.0 * inverse_adaptive(p))
    copies = []
    for i in range(STORES):
        rows = pl.ds(i * chunk, chunk)
        y = turn(work[0, rows, :], work[1, rows, :], x_wide, p_wide, d[i * chunk : (i + 1) * chunk])
        for which, out in enumerate((out_upper, out_lower)):
            stage[which, rows, :] = y[which]
            copies.append(pltpu.make_async_copy(stage.at[which, rows], out.at[rows], sems.at[which, i]))
            copies[-1].start()
    for copy in copies:
        copy.wait()


def shards(n_row, n_col, upper_blocks, lower_blocks):
    depth, width = upper_blocks.shape
    half = width // 2
    n_line = n_row // 2
    out = jax.ShapeDtypeStruct((depth, width), F32)
    dma = pltpu.SemaphoreType.DMA
    flag = pltpu.SemaphoreType.REGULAR
    work, p = pl.pallas_call(
        functools.partial(kernel, n_row, n_col),
        out_shape=(pltpu.VMEM((3, depth, width), F32), pltpu.VMEM((width, width), F32)),
        in_specs=[pl.BlockSpec(memory_space=pl.ANY)] * 2,
        out_specs=(pl.BlockSpec(memory_space=pltpu.VMEM),) * 2,
        scratch_shapes=[
            pltpu.VMEM((2, depth, width), F32),
            pltpu.VMEM((2, RELAYED * (depth // 8), width), F32),
            pltpu.VMEM((2, depth, width), F32),
            pltpu.VMEM((3, depth, width), F32),
            pltpu.VMEM((ROUNDS, 2, half + 8, width), F32),
            pltpu.VMEM((2, half + 8, width), F32),
            pltpu.VMEM((ROUNDS, half + 8, width), F32),
            pltpu.VMEM((n_line - 1, half + 8, width), F32),
            pltpu.VMEM((n_line, half + 8, width), F32),
            pltpu.VMEM((ROUNDS, 2, half + 8, width), F32),
            pltpu.VMEM((2, half + 8, width), F32),
            pltpu.VMEM((2, half + 8, width), F32),
            dma((2,)),
            dma((2,)),
            dma((n_line - 1,)),
            dma((n_line - 1,)),
            dma((n_line,)),
            dma((n_line,)),
            dma((ROUNDS,)),
            dma((ROUNDS,)),
            dma((2,)),
            dma((2,)),
            dma((2,)),
            dma((2,)),
            dma((2, 2)),
            dma((2, 2)),
            dma((2, 2)),
            dma((2, 2)),
            dma((SHIFTS,)),
            dma((SHIFTS,)),
            dma((1,)),
            dma((1,)),
            dma((3,)),
            dma((3,)),
            dma((2, LOADS)),
            flag((max(n_line - 2, 1),)),
            flag((max(n_line - 2, 1),)),
        ],
        compiler_params=pltpu.CompilerParams(collective_id=0, has_side_effects=True),
    )(upper_blocks, lower_blocks)
    return pl.pallas_call(
        finish,
        out_shape=(out, out),
        in_specs=[pl.BlockSpec(memory_space=pltpu.VMEM)] * 2,
        out_specs=(pl.BlockSpec(memory_space=pl.ANY),) * 2,
        scratch_shapes=[pltpu.VMEM((2, depth, width), F32), dma((2, STORES))],
    )(*(pltpu.with_memory_space_constraint(x, pltpu.VMEM) for x in (work, p)))


def solution(mesh):
    placed = (P("row", "col"), P("row", "col"))
    return jax.shard_map(
        functools.partial(shards, mesh.shape["row"], mesh.shape["col"]),
        mesh=mesh,
        in_specs=placed,
        out_specs=(P("row", "col"), P("row", "col")),
        check_vma=False,
    )
```

```python
import functools

import jax
import jax.numpy as jnp
from jax import lax
from jax.experimental import pallas as pl
from jax.experimental.pallas import tpu as pltpu
from jax.sharding import PartitionSpec as P

ROUNDS = 2
LOADS = 1
RELAYED = 5
RELAYED_FIRST = 5
RAW_FROM = 2
RECEIVED_FIRST = 4
SHIFTS = 1
EXACT_ABOVE = 1.0
STORES = 4
MESH = pl.DeviceIdType.MESH
F32 = jnp.float32
BF16 = jnp.bfloat16


def split(x):
    high = x.astype(BF16)
    low = (x - high.astype(F32)).astype(BF16)
    return high, low


def split_three(x):
    high = x.astype(BF16)
    rest = x - high.astype(F32)
    middle = rest.astype(BF16)
    return high, middle, (rest - middle.astype(F32)).astype(BF16)


def fast_dot(a, b):
    return jnp.dot(a, b, preferred_element_type=F32)


def exact_dot(a, b):
    width = b.shape[1]
    (a0, a1, a2), (b0, b1, b2) = split_three(a), split_three(b)
    upper = jnp.concatenate([b0, b1], axis=1)
    lower = jnp.concatenate([b1, b0], axis=1)
    large = fast_dot(jnp.concatenate([a0, a1], axis=1), jnp.concatenate([upper, lower], axis=0))
    small = fast_dot(jnp.concatenate([a0, a2], axis=1), jnp.concatenate([b2, b0], axis=0))
    return large[:, :width] + (large[:, width:] + small)


def wide(b):
    both = jnp.concatenate(split(b), axis=1)
    return jnp.concatenate([both, both], axis=0)


def tall_dot(a, b_wide):
    width = a.shape[1]
    y = fast_dot(jnp.concatenate(split(a), axis=1), b_wide)
    return y[:, :width] + y[:, width:]


def gram(upper, lower):
    width = upper.shape[1]
    left = jnp.concatenate(split(upper), axis=1)
    right = jnp.concatenate(split(lower), axis=1)
    q = lax.dot_general(
        left, right, (((0,), (0,)), ((), ())), preferred_element_type=F32
    )
    return q[:width, :width] + (q[:width, width:] + q[width:, :width])


def identity(width):
    rows = lax.broadcasted_iota(jnp.int32, (width, width), 0)
    lanes = lax.broadcasted_iota(jnp.int32, (width, width), 1)
    return (rows == lanes).astype(F32)


def shrink(spread):
    square = spread * spread
    gain = 2.0 / (2.0 - square)
    return gain, 0.5 * square * gain


def step_count(width):
    square = (width / 4.0) ** 2
    spread = 0.5 * square / (1.0 + 0.5 * square)
    steps = 0
    while spread > 1e-3:
        spread = shrink(spread)[1]
        steps += 1
    return steps


def quick_dot(a, b):
    return tall_dot(a, wide(b))


def correct(s, x):
    e = (identity(x.shape[0]) - x) - exact_dot(s, x)
    return x + quick_dot(x, e)


def inverse(p):
    width = p.shape[0]
    eye = identity(width)
    s = exact_dot(p, p.T)
    total = jnp.sum(jnp.sum(p * p, axis=0, keepdims=True), axis=1, keepdims=True)
    total = jnp.broadcast_to(total, (1, width))
    scale = 1.0 / (1.0 + 0.5 * total)
    spread = 0.5 * total * scale
    e = spread * eye - scale * s
    x = None
    steps = step_count(width)
    for step in range(steps):
        gain, spread = shrink(spread)
        if step == 0:
            x = (gain * scale) * (eye + e)
        else:
            x = gain * (x + quick_dot(x, e))
        if step < steps - 1:
            e = gain * quick_dot(e, e) - spread * eye
    return correct(s, x)


def inverse_adaptive(p):
    width = p.shape[0]
    eye = identity(width)
    s = exact_dot(p, p.T)
    bound = 1.0001 * jnp.max(jnp.sum(jnp.abs(s), axis=0, keepdims=True))
    scale = 1.0 / (1.0 + 0.5 * bound)
    spread = 0.5 * bound * scale
    squared = (scale * scale) * exact_dot(s, s) + (spread * spread) * eye - (2.0 * spread * scale) * s
    gain, smaller = shrink(spread)
    x = (gain * scale) * ((1.0 + spread) * eye - scale * s)

    def body(state):
        x, e, spread = state
        gain, spread = shrink(spread)
        return gain * (x + quick_dot(x, e)), gain * quick_dot(e, e) - spread * eye, spread

    x = lax.while_loop(lambda state: state[2] > 3e-6, body, (x, gain * squared - smaller * eye, smaller))[0]
    return lax.cond(bound > EXACT_ABOVE, lambda: correct(s, x), lambda: x)


def turn(upper, lower, x_wide, p_wide, d):
    v = tall_dot(d, x_wide)
    return v - upper, lower + tall_dot(v, p_wide)


def kernel(
    n_row, n_col, upper_hbm, lower_hbm, work, out_p,
    loaded, relayed, swapped, home, gram_out, gram_in, line_out, line_in, cross_in, totals, others, besides,
    gram_send, gram_recv, line_send, line_recv, cross_send, cross_recv,
    pair_send, pair_recv, other_send, other_recv, beside_send, beside_recv,
    relay_send, relay_recv, swap_send, swap_recv, shift_send, shift_recv, carry_send, carry_recv, move_send, move_recv, load_sem, up_sem, down_sem,
):
    depth, width = upper_hbm.shape
    half = width // 2
    n_line = n_row // 2
    row_total = float(depth * n_row)
    row, col = lax.axis_index("row"), lax.axis_index("col")
    core = lax.rem(row, 2)
    chip_row = row - core
    place = chip_row // 2
    partner = chip_row + 1 - core
    odd = lax.rem(col, 2)
    even = 1 - odd
    beside = col + 1 - 2 * odd
    ahead = lax.rem(col + 2, n_col)
    behind = lax.rem(col + n_col - 2, n_col)
    shift_to = ahead + even * (behind - ahead)
    carry_to = ahead + odd * (behind - ahead)
    has_prev, has_next = place > 0, place < n_line - 1
    early = RELAYED * (depth // 8)
    early_rows = pl.ds(0, early)
    line = pl.ds(0, half + 1)

    def line_row(k):
        return lax.rem(row + 2 * k, n_row)

    def piece(i, count, first=0, last=None):
        size = ((depth if last is None else last) - first) // count
        return pl.ds(first + i * size, size)

    loads = []
    for i in range(LOADS):
        rows = piece(i, LOADS)
        for which, ref in enumerate((upper_hbm, lower_hbm)):
            loads.append(pltpu.make_async_copy(ref.at[rows], loaded.at[which, rows], load_sem.at[which, i]))
            loads[-1].start()
    barrier = pltpu.get_barrier_semaphore()

    def greet(r, c):
        pl.semaphore_signal(barrier, inc=1, device_id={"row": r, "col": c}, device_id_type=MESH)

    greeted = [(chip_row, beside), (chip_row + 1, beside), (partner, col)]
    for c in [ahead] + ([] if n_col == 4 else [behind]):
        greeted += [(chip_row, c), (chip_row + 1, c)]
    for r, c in greeted:
        greet(r, c)

    @pl.when(has_prev)
    def _():
        greet(row - 2, col)

    @pl.when(has_next)
    def _():
        greet(row + 2, col)

    pl.semaphore_wait(barrier, len(greeted) + has_prev.astype(jnp.int32) + has_next.astype(jnp.int32))

    def remote(src, dst, send, recv, r, c):
        return pltpu.make_async_remote_copy(
            src_ref=src, dst_ref=dst, send_sem=send, recv_sem=recv,
            device_id={"row": r, "col": c}, device_id_type=MESH,
        )

    pending = []

    def start(copy):
        copy.start()
        pending.append(copy)
        return copy

    def send_raw(i, first, last, dst, send, recv, c):
        rows = pl.ds(first * (depth // 8), (last - first) * (depth // 8))
        return [
            start(remote(ref.at[rows], dst.at[which, rows], send.at[which, i], recv.at[which, i], row, c))
            for which, ref in enumerate((upper_hbm, lower_hbm))
        ]

    def relay(i, first, last):
        return send_raw(i, first, last, relayed, relay_send, relay_recv, shift_to)

    def swap(i, first, last):
        return send_raw(i, first, last, swapped, swap_send, swap_recv, beside)

    relays = relay(0, 0, RELAYED_FIRST)
    swaps = swap(0, RAW_FROM, 8)

    def put_statistics(index, g, upper_sums, lower_sums):
        for k, sums in enumerate((upper_sums, lower_sums)):
            gram_out[index, k, :half, :] = g[k * half : (k + 1) * half]
            gram_out[index, k, half : half + 1, :] = sums

    def share(index, total):
        totals[index, core, line, :] = total
        return start(
            remote(
                totals.at[index, core, line], totals.at[index, core, line],
                pair_send.at[index], pair_recv.at[index], partner, col,
            )
        )

    def reduce_line(own):
        line_out[0, line, :] = own
        copies = []
        for k in range(1, n_line):
            copies.append(
                start(
                    remote(
                        line_out.at[0, line], line_in.at[k - 1, line],
                        line_send.at[k - 1], line_recv.at[k - 1], line_row(k), col,
                    )
                )
            )
        total = own
        for k in range(1, n_line):
            copies[k - 1].wait_recv()
            total = total + line_in[k - 1, line, :]
        return total

    def coupling(read):
        both_halves = jnp.concatenate([read(k, slice(0, half)) for k in range(2)], axis=0)
        a_row, b = (read(k, slice(half, half + 1)) / row_total for k in range(2))
        a = jnp.broadcast_to(a_row, (width, width)).T
        gap, both = a - b, a + b
        factor = -gap / (2.0 * gap * gap + 0.5 * both * both + 1e-05)
        return (both_halves / row_total) * factor

    def statistics(index, pieces, fetch):
        g, upper_sums, lower_sums = 0.0, 0.0, 0.0
        for i, rows in enumerate(pieces):
            upper, lower = fetch(i, rows)
            g = g + gram(upper, lower)
            upper_sums = upper_sums + jnp.sum(upper * upper, axis=0, keepdims=True)
            lower_sums = lower_sums + jnp.sum(lower * lower, axis=0, keepdims=True)
        put_statistics(index, g, upper_sums, lower_sums)

    def fetch_loaded(i, rows):
        loads[2 * i].wait()
        loads[2 * i + 1].wait()
        return loaded[0, rows, :], loaded[1, rows, :]

    statistics(0, [piece(i, LOADS) for i in range(LOADS)], fetch_loaded)
    copy = start(
        remote(gram_out.at[0, 1 - core, line], gram_in.at[0, line], gram_send.at[0], gram_recv.at[0], partner, col)
    )

    for s in range(n_line - 2):

        @pl.when(jnp.logical_and(has_next, place > s))
        def _():
            pl.semaphore_signal(up_sem.at[s], inc=1, device_id={"row": row + 2, "col": col}, device_id_type=MESH)

        @pl.when(jnp.logical_and(has_prev, place < n_line - 1 - s))
        def _():
            pl.semaphore_signal(down_sem.at[s], inc=1, device_id={"row": row - 2, "col": col}, device_id_type=MESH)

        @pl.when(place > s + 1)
        def _():
            pl.semaphore_wait(up_sem.at[s], 1)

        @pl.when(place < n_line - 2 - s)
        def _():
            pl.semaphore_wait(down_sem.at[s], 1)

    copy.wait_recv()
    own_copy = share(0, reduce_line(gram_out[0, core, line, :] + gram_in[0, line, :]))
    for k in range(2):
        start(
            remote(
                totals.at[0, core, line], others.at[core, line], other_send.at[k], other_recv.at[core],
                chip_row + k, shift_to,
            )
        )
    for k in range(2):
        start(
            remote(
                totals.at[0, core, line], besides.at[core, line], beside_send.at[k], beside_recv.at[core],
                chip_row + k, beside,
            )
        )
    if RELAYED > RELAYED_FIRST:
        relays += relay(1, RELAYED_FIRST, RELAYED)
    own_copy.wait_recv()
    p = coupling(lambda k, rows: totals[0, k, rows, :])
    upper, lower = loaded[0], loaded[1]
    d = upper - tall_dot(lower, wide(p.T))
    x_wide, p_wide = wide(2.0 * inverse(p)), wide(p)
    upper_slot, lower_slot = 2 - 2 * even, 1 + even

    def place_turned(rows, size):
        new_upper, new_lower = turn(
            loaded[0, rows, :], loaded[1, rows, :], x_wide, p_wide, d[rows.start : rows.start + size]
        )
        home[upper_slot, rows, :] = new_upper
        home[lower_slot, rows, :] = new_lower

    def eighths(first, last):
        return pl.ds(first * (depth // 8), (last - first) * (depth // 8))

    move_rows = [eighths(0, RAW_FROM), eighths(0, RECEIVED_FIRST), eighths(RECEIVED_FIRST, RELAYED)]

    def move_copy(i, slot):
        return remote(
            home.at[slot, move_rows[i]], work.at[slot, move_rows[i]],
            move_send.at[i], move_recv.at[i], row, beside,
        )

    shifts = []
    shift_rows = [piece(i, SHIFTS, early) for i in range(SHIFTS)]
    for i, rows in enumerate(shift_rows):
        place_turned(rows, rows.size)
        shifts.append(
            start(
                remote(
                    home.at[2, rows], home.at[even, rows], shift_send.at[i], shift_recv.at[i],
                    row, shift_to,
                )
            )
        )
    place_turned(early_rows, early)
    start(move_copy(0, odd))
    for k in range(2):
        remote(
            totals.at[0, k, line], others.at[k, line], other_send.at[k], other_recv.at[k], row, shift_to
        ).wait_recv()
    p = coupling(lambda k, rows: others[k, rows, :])
    for copy in relays:
        copy.wait_recv()
    upper, lower = relayed[0], relayed[1]
    d = upper - tall_dot(lower, wide(p.T))
    new_upper, new_lower = turn(upper, lower, wide(2.0 * inverse(p)), wide(p), d)
    home[2 * even, early_rows, :] = new_upper
    home[2 - even, early_rows, :] = new_lower

    start(move_copy(1, even))

    def fetch_shifted(i, rows):
        if i > 0:
            shifts[i - 1].wait_recv()
        return home[0, rows, :], home[1, rows, :]

    statistics(1, [early_rows] + shift_rows, fetch_shifted)
    copy = start(
        remote(gram_out.at[1, 1 - core, line], gram_in.at[1, line], gram_send.at[1], gram_recv.at[1], partner, col)
    )
    copy.wait_recv()
    line_out[1, line, :] = gram_out[1, core, line, :] + gram_in[1, line, :]
    crossing = [
        start(
            remote(
                line_out.at[1, line], cross_in.at[k, line], cross_send.at[k], cross_recv.at[k], line_row(k), beside
            )
        )
        for k in range(n_line)
    ]
    start(move_copy(2, even))
    for k in range(2):
        remote(
            totals.at[0, k, line], besides.at[k, line], beside_send.at[k], beside_recv.at[k], row, beside
        ).wait_recv()
    p = coupling(lambda k, rows: besides[k, rows, :])
    back, p_wide, x_wide = wide(p.T), wide(p), wide(2.0 * inverse(p))
    for copy in swaps:
        copy.wait_recv()

    def place_swapped(rows):
        upper, lower = swapped[0, rows, :], swapped[1, rows, :]
        new_upper, new_lower = turn(upper, lower, x_wide, p_wide, upper - tall_dot(lower, back))
        work[2 - 2 * odd, rows, :] = new_upper
        work[1 + odd, rows, :] = new_lower

    late_rows = eighths(RELAYED, 8)
    place_swapped(late_rows)
    carried = start(
        remote(
            work.at[2, late_rows], work.at[odd, late_rows], carry_send.at[0], carry_recv.at[0], row, carry_to
        )
    )
    place_swapped(eighths(RAW_FROM, RELAYED))
    total = 0.0
    for k in range(n_line):
        crossing[k].wait_recv()
        total = total + cross_in[k, line, :]
    share(1, total).wait_recv()
    out_p[...] = coupling(lambda k, rows: totals[1, k, rows, :])
    carried.wait_recv()
    for i, slot in enumerate((even, odd, odd)):
        move_copy(i, slot).wait_recv()
    for copy in pending:
        copy.wait_send()


def finish(work, p_ref, out_upper, out_lower, stage, sems):
    depth, width = out_upper.shape
    chunk = depth // STORES
    p = p_ref[...]
    d = work[0] - tall_dot(work[1], wide(p.T))
    p_wide, x_wide = wide(p), wide(2.0 * inverse_adaptive(p))
    copies = []
    for i in range(STORES):
        rows = pl.ds(i * chunk, chunk)
        y = turn(work[0, rows, :], work[1, rows, :], x_wide, p_wide, d[i * chunk : (i + 1) * chunk])
        for which, out in enumerate((out_upper, out_lower)):
            stage[which, rows, :] = y[which]
            copies.append(pltpu.make_async_copy(stage.at[which, rows], out.at[rows], sems.at[which, i]))
            copies[-1].start()
    for copy in copies:
        copy.wait()


def shards(n_row, n_col, upper_blocks, lower_blocks):
    depth, width = upper_blocks.shape
    half = width // 2
    n_line = n_row // 2
    out = jax.ShapeDtypeStruct((depth, width), F32)
    dma = pltpu.SemaphoreType.DMA
    flag = pltpu.SemaphoreType.REGULAR
    work, p = pl.pallas_call(
        functools.partial(kernel, n_row, n_col),
        out_shape=(pltpu.VMEM((3, depth, width), F32), pltpu.VMEM((width, width), F32)),
        in_specs=[pl.BlockSpec(memory_space=pl.ANY)] * 2,
        out_specs=(pl.BlockSpec(memory_space=pltpu.VMEM),) * 2,
        scratch_shapes=[
            pltpu.VMEM((2, depth, width), F32),
            pltpu.VMEM((2, RELAYED * (depth // 8), width), F32),
            pltpu.VMEM((2, depth, width), F32),
            pltpu.VMEM((3, depth, width), F32),
            pltpu.VMEM((ROUNDS, 2, half + 8, width), F32),
            pltpu.VMEM((2, half + 8, width), F32),
            pltpu.VMEM((ROUNDS, half + 8, width), F32),
            pltpu.VMEM((n_line - 1, half + 8, width), F32),
            pltpu.VMEM((n_line, half + 8, width), F32),
            pltpu.VMEM((ROUNDS, 2, half + 8, width), F32),
            pltpu.VMEM((2, half + 8, width), F32),
            pltpu.VMEM((2, half + 8, width), F32),
            dma((2,)),
            dma((2,)),
            dma((n_line - 1,)),
            dma((n_line - 1,)),
            dma((n_line,)),
            dma((n_line,)),
            dma((ROUNDS,)),
            dma((ROUNDS,)),
            dma((2,)),
            dma((2,)),
            dma((2,)),
            dma((2,)),
            dma((2, 2)),
            dma((2, 2)),
            dma((2, 2)),
            dma((2, 2)),
            dma((SHIFTS,)),
            dma((SHIFTS,)),
            dma((1,)),
            dma((1,)),
            dma((3,)),
            dma((3,)),
            dma((2, LOADS)),
            flag((max(n_line - 2, 1),)),
            flag((max(n_line - 2, 1),)),
        ],
        compiler_params=pltpu.CompilerParams(collective_id=0, has_side_effects=True),
    )(upper_blocks, lower_blocks)
    return pl.pallas_call(
        finish,
        out_shape=(out, out),
        in_specs=[pl.BlockSpec(memory_space=pltpu.VMEM)] * 2,
        out_specs=(pl.BlockSpec(memory_space=pl.ANY),) * 2,
        scratch_shapes=[pltpu.VMEM((2, depth, width), F32), dma((2, STORES))],
    )(*(pltpu.with_memory_space_constraint(x, pltpu.VMEM) for x in (work, p)))


def solution(mesh):
    placed = (P("row", "col"), P("row", "col"))
    return jax.shard_map(
        functools.partial(shards, mesh.shape["row"], mesh.shape["col"]),
        mesh=mesh,
        in_specs=placed,
        out_specs=(P("row", "col"), P("row", "col")),
        check_vma=False,
    )
```

```python
import functools

import jax
import jax.numpy as jnp
from jax import lax
from jax.experimental import pallas as pl
from jax.experimental.pallas import tpu as pltpu
from jax.sharding import PartitionSpec as P

ROUNDS = 2
LOADS = 1
RELAYED = 5
RELAYED_FIRST = 5
RAW_FROM = 2
RECEIVED_FIRST = 4
SHIFTS = 1
EXACT_ABOVE = 1.0
STORES = 4
MESH = pl.DeviceIdType.MESH
F32 = jnp.float32
BF16 = jnp.bfloat16


def split(x):
    high = x.astype(BF16)
    low = (x - high.astype(F32)).astype(BF16)
    return high, low


def split_three(x):
    high = x.astype(BF16)
    rest = x - high.astype(F32)
    middle = rest.astype(BF16)
    return high, middle, (rest - middle.astype(F32)).astype(BF16)


def fast_dot(a, b):
    return jnp.dot(a, b, preferred_element_type=F32)


def exact_dot(a, b):
    width = b.shape[1]
    (a0, a1, a2), (b0, b1, b2) = split_three(a), split_three(b)
    upper = jnp.concatenate([b0, b1], axis=1)
    lower = jnp.concatenate([b1, b0], axis=1)
    large = fast_dot(jnp.concatenate([a0, a1], axis=1), jnp.concatenate([upper, lower], axis=0))
    small = fast_dot(jnp.concatenate([a0, a2], axis=1), jnp.concatenate([b2, b0], axis=0))
    return large[:, :width] + (large[:, width:] + small)


def wide(b):
    both = jnp.concatenate(split(b), axis=1)
    return jnp.concatenate([both, both], axis=0)


def tall_dot(a, b_wide):
    width = a.shape[1]
    y = fast_dot(jnp.concatenate(split(a), axis=1), b_wide)
    return y[:, :width] + y[:, width:]


def gram(upper, lower):
    width = upper.shape[1]
    left = jnp.concatenate(split(upper), axis=1)
    right = jnp.concatenate(split(lower), axis=1)
    q = lax.dot_general(
        left, right, (((0,), (0,)), ((), ())), preferred_element_type=F32
    )
    return q[:width, :width] + (q[:width, width:] + q[width:, :width])


def identity(width):
    rows = lax.broadcasted_iota(jnp.int32, (width, width), 0)
    lanes = lax.broadcasted_iota(jnp.int32, (width, width), 1)
    return (rows == lanes).astype(F32)


def shrink(spread):
    square = spread * spread
    gain = 2.0 / (2.0 - square)
    return gain, 0.5 * square * gain


def step_count(width):
    square = (width / 4.0) ** 2
    spread = 0.5 * square / (1.0 + 0.5 * square)
    steps = 0
    while spread > 1e-3:
        spread = shrink(spread)[1]
        steps += 1
    return steps


def quick_dot(a, b):
    return tall_dot(a, wide(b))


def correct(s, x):
    e = (identity(x.shape[0]) - x) - exact_dot(s, x)
    return x + quick_dot(x, e)


def inverse(p):
    width = p.shape[0]
    eye = identity(width)
    s = exact_dot(p, p.T)
    total = jnp.sum(jnp.sum(p * p, axis=0, keepdims=True), axis=1, keepdims=True)
    total = jnp.broadcast_to(total, (1, width))
    scale = 1.0 / (1.0 + 0.5 * total)
    spread = 0.5 * total * scale
    e = spread * eye - scale * s
    x = None
    steps = step_count(width)
    for step in range(steps):
        gain, spread = shrink(spread)
        if step == 0:
            x = (gain * scale) * (eye + e)
        else:
            x = gain * (x + quick_dot(x, e))
        if step < steps - 1:
            e = gain * quick_dot(e, e) - spread * eye
    return correct(s, x)


def inverse_adaptive(p):
    width = p.shape[0]
    eye = identity(width)
    s = exact_dot(p, p.T)
    bound = 1.0001 * jnp.max(jnp.sum(jnp.abs(s), axis=0, keepdims=True))
    scale = 1.0 / (1.0 + 0.5 * bound)
    spread = 0.5 * bound * scale
    squared = (scale * scale) * exact_dot(s, s) + (spread * spread) * eye - (2.0 * spread * scale) * s
    gain, smaller = shrink(spread)
    x = (gain * scale) * ((1.0 + spread) * eye - scale * s)

    def body(state):
        x, e, spread = state
        gain, spread = shrink(spread)
        return gain * (x + quick_dot(x, e)), gain * quick_dot(e, e) - spread * eye, spread

    state = body((x, gain * squared - smaller * eye, smaller))
    x = lax.while_loop(lambda state: state[2] > 3e-6, body, state)[0]
    return lax.cond(bound > EXACT_ABOVE, lambda: correct(s, x), lambda: x)


def turn(upper, lower, x_wide, p_wide, d):
    v = tall_dot(d, x_wide)
    return v - upper, lower + tall_dot(v, p_wide)


def kernel(
    n_row, n_col, upper_hbm, lower_hbm, work, out_p,
    loaded, relayed, swapped, home, gram_out, gram_in, line_out, line_in, cross_in, totals, others, besides,
    gram_send, gram_recv, line_send, line_recv, cross_send, cross_recv,
    pair_send, pair_recv, other_send, other_recv, beside_send, beside_recv,
    relay_send, relay_recv, swap_send, swap_recv, shift_send, shift_recv, carry_send, carry_recv, move_send, move_recv, load_sem, up_sem, down_sem,
):
    depth, width = upper_hbm.shape
    half = width // 2
    n_line = n_row // 2
    row_total = float(depth * n_row)
    row, col = lax.axis_index("row"), lax.axis_index("col")
    core = lax.rem(row, 2)
    chip_row = row - core
    place = chip_row // 2
    partner = chip_row + 1 - core
    odd = lax.rem(col, 2)
    even = 1 - odd
    beside = col + 1 - 2 * odd
    ahead = lax.rem(col + 2, n_col)
    behind = lax.rem(col + n_col - 2, n_col)
    shift_to = ahead + even * (behind - ahead)
    carry_to = ahead + odd * (behind - ahead)
    has_prev, has_next = place > 0, place < n_line - 1
    early = RELAYED * (depth // 8)
    early_rows = pl.ds(0, early)
    line = pl.ds(0, half + 1)

    def line_row(k):
        return lax.rem(row + 2 * k, n_row)

    def piece(i, count, first=0, last=None):
        size = ((depth if last is None else last) - first) // count
        return pl.ds(first + i * size, size)

    loads = []
    for i in range(LOADS):
        rows = piece(i, LOADS)
        for which, ref in enumerate((upper_hbm, lower_hbm)):
            loads.append(pltpu.make_async_copy(ref.at[rows], loaded.at[which, rows], load_sem.at[which, i]))
            loads[-1].start()
    barrier = pltpu.get_barrier_semaphore()

    def greet(r, c):
        pl.semaphore_signal(barrier, inc=1, device_id={"row": r, "col": c}, device_id_type=MESH)

    greeted = [(chip_row, beside), (chip_row + 1, beside), (partner, col)]
    for c in [ahead] + ([] if n_col == 4 else [behind]):
        greeted += [(chip_row, c), (chip_row + 1, c)]
    for r, c in greeted:
        greet(r, c)

    @pl.when(has_prev)
    def _():
        greet(row - 2, col)

    @pl.when(has_next)
    def _():
        greet(row + 2, col)

    pl.semaphore_wait(barrier, len(greeted) + has_prev.astype(jnp.int32) + has_next.astype(jnp.int32))

    def remote(src, dst, send, recv, r, c):
        return pltpu.make_async_remote_copy(
            src_ref=src, dst_ref=dst, send_sem=send, recv_sem=recv,
            device_id={"row": r, "col": c}, device_id_type=MESH,
        )

    pending = []

    def start(copy):
        copy.start()
        pending.append(copy)
        return copy

    def send_raw(i, first, last, dst, send, recv, c):
        rows = pl.ds(first * (depth // 8), (last - first) * (depth // 8))
        return [
            start(remote(ref.at[rows], dst.at[which, rows], send.at[which, i], recv.at[which, i], row, c))
            for which, ref in enumerate((upper_hbm, lower_hbm))
        ]

    def relay(i, first, last):
        return send_raw(i, first, last, relayed, relay_send, relay_recv, shift_to)

    def swap(i, first, last):
        return send_raw(i, first, last, swapped, swap_send, swap_recv, beside)

    relays = relay(0, 0, RELAYED_FIRST)
    swaps = swap(0, RAW_FROM, 8)

    def put_statistics(index, g, upper_sums, lower_sums):
        for k, sums in enumerate((upper_sums, lower_sums)):
            gram_out[index, k, :half, :] = g[k * half : (k + 1) * half]
            gram_out[index, k, half : half + 1, :] = sums

    def share(index, total):
        totals[index, core, line, :] = total
        return start(
            remote(
                totals.at[index, core, line], totals.at[index, core, line],
                pair_send.at[index], pair_recv.at[index], partner, col,
            )
        )

    def reduce_line(own):
        line_out[0, line, :] = own
        copies = []
        for k in range(1, n_line):
            copies.append(
                start(
                    remote(
                        line_out.at[0, line], line_in.at[k - 1, line],
                        line_send.at[k - 1], line_recv.at[k - 1], line_row(k), col,
                    )
                )
            )
        total = own
        for k in range(1, n_line):
            copies[k - 1].wait_recv()
            total = total + line_in[k - 1, line, :]
        return total

    def coupling(read):
        both_halves = jnp.concatenate([read(k, slice(0, half)) for k in range(2)], axis=0)
        a_row, b = (read(k, slice(half, half + 1)) / row_total for k in range(2))
        a = jnp.broadcast_to(a_row, (width, width)).T
        gap, both = a - b, a + b
        factor = -gap / (2.0 * gap * gap + 0.5 * both * both + 1e-05)
        return (both_halves / row_total) * factor

    def statistics(index, pieces, fetch):
        g, upper_sums, lower_sums = 0.0, 0.0, 0.0
        for i, rows in enumerate(pieces):
            upper, lower = fetch(i, rows)
            g = g + gram(upper, lower)
            upper_sums = upper_sums + jnp.sum(upper * upper, axis=0, keepdims=True)
            lower_sums = lower_sums + jnp.sum(lower * lower, axis=0, keepdims=True)
        put_statistics(index, g, upper_sums, lower_sums)

    def fetch_loaded(i, rows):
        loads[2 * i].wait()
        loads[2 * i + 1].wait()
        return loaded[0, rows, :], loaded[1, rows, :]

    statistics(0, [piece(i, LOADS) for i in range(LOADS)], fetch_loaded)
    copy = start(
        remote(gram_out.at[0, 1 - core, line], gram_in.at[0, line], gram_send.at[0], gram_recv.at[0], partner, col)
    )

    for s in range(n_line - 2):

        @pl.when(jnp.logical_and(has_next, place > s))
        def _():
            pl.semaphore_signal(up_sem.at[s], inc=1, device_id={"row": row + 2, "col": col}, device_id_type=MESH)

        @pl.when(jnp.logical_and(has_prev, place < n_line - 1 - s))
        def _():
            pl.semaphore_signal(down_sem.at[s], inc=1, device_id={"row": row - 2, "col": col}, device_id_type=MESH)

        @pl.when(place > s + 1)
        def _():
            pl.semaphore_wait(up_sem.at[s], 1)

        @pl.when(place < n_line - 2 - s)
        def _():
            pl.semaphore_wait(down_sem.at[s], 1)

    copy.wait_recv()
    own_copy = share(0, reduce_line(gram_out[0, core, line, :] + gram_in[0, line, :]))
    for k in range(2):
        start(
            remote(
                totals.at[0, core, line], others.at[core, line], other_send.at[k], other_recv.at[core],
                (row, partner)[k], shift_to,
            )
        )
    for k in range(2):
        start(
            remote(
                totals.at[0, core, line], besides.at[core, line], beside_send.at[k], beside_recv.at[core],
                (row, partner)[k], beside,
            )
        )
    if RELAYED > RELAYED_FIRST:
        relays += relay(1, RELAYED_FIRST, RELAYED)
    own_copy.wait_recv()
    p = coupling(lambda k, rows: totals[0, k, rows, :])
    upper, lower = loaded[0], loaded[1]
    d = upper - tall_dot(lower, wide(p.T))
    x_wide, p_wide = wide(2.0 * inverse(p)), wide(p)
    upper_slot, lower_slot = 2 - 2 * even, 1 + even

    def place_turned(rows, size):
        new_upper, new_lower = turn(
            loaded[0, rows, :], loaded[1, rows, :], x_wide, p_wide, d[rows.start : rows.start + size]
        )
        home[upper_slot, rows, :] = new_upper
        home[lower_slot, rows, :] = new_lower

    def eighths(first, last):
        return pl.ds(first * (depth // 8), (last - first) * (depth // 8))

    move_rows = [eighths(0, RAW_FROM), eighths(0, RECEIVED_FIRST), eighths(RECEIVED_FIRST, RELAYED)]

    def move_copy(i, slot):
        return remote(
            home.at[slot, move_rows[i]], work.at[slot, move_rows[i]],
            move_send.at[i], move_recv.at[i], row, beside,
        )

    shifts = []
    shift_rows = [piece(i, SHIFTS, early) for i in range(SHIFTS)]
    for i, rows in enumerate(shift_rows):
        place_turned(rows, rows.size)
        shifts.append(
            start(
                remote(
                    home.at[2, rows], home.at[even, rows], shift_send.at[i], shift_recv.at[i],
                    row, shift_to,
                )
            )
        )
    place_turned(early_rows, early)
    start(move_copy(0, odd))
    for k in range(2):
        remote(
            totals.at[0, k, line], others.at[k, line], other_send.at[k], other_recv.at[k], row, shift_to
        ).wait_recv()
    p = coupling(lambda k, rows: others[k, rows, :])
    for copy in relays:
        copy.wait_recv()
    upper, lower = relayed[0], relayed[1]
    d = upper - tall_dot(lower, wide(p.T))
    new_upper, new_lower = turn(upper, lower, wide(2.0 * inverse(p)), wide(p), d)
    home[2 * even, early_rows, :] = new_upper
    home[2 - even, early_rows, :] = new_lower

    start(move_copy(1, even))

    def fetch_shifted(i, rows):
        if i > 0:
            shifts[i - 1].wait_recv()
        return home[0, rows, :], home[1, rows, :]

    statistics(1, [early_rows] + shift_rows, fetch_shifted)
    copy = start(
        remote(gram_out.at[1, 1 - core, line], gram_in.at[1, line], gram_send.at[1], gram_recv.at[1], partner, col)
    )
    copy.wait_recv()
    line_out[1, line, :] = gram_out[1, core, line, :] + gram_in[1, line, :]
    crossing = [
        start(
            remote(
                line_out.at[1, line], cross_in.at[k, line], cross_send.at[k], cross_recv.at[k], line_row(k), beside
            )
        )
        for k in range(n_line)
    ]
    start(move_copy(2, even))
    for k in range(2):
        remote(
            totals.at[0, k, line], besides.at[k, line], beside_send.at[k], beside_recv.at[k], row, beside
        ).wait_recv()
    p = coupling(lambda k, rows: besides[k, rows, :])
    back, p_wide, x_wide = wide(p.T), wide(p), wide(2.0 * inverse(p))
    for copy in swaps:
        copy.wait_recv()

    def place_swapped(rows):
        upper, lower = swapped[0, rows, :], swapped[1, rows, :]
        new_upper, new_lower = turn(upper, lower, x_wide, p_wide, upper - tall_dot(lower, back))
        work[2 - 2 * odd, rows, :] = new_upper
        work[1 + odd, rows, :] = new_lower

    late_rows = eighths(RELAYED, 8)
    place_swapped(late_rows)
    carried = start(
        remote(
            work.at[2, late_rows], work.at[odd, late_rows], carry_send.at[0], carry_recv.at[0], row, carry_to
        )
    )
    place_swapped(eighths(RAW_FROM, RELAYED))
    total = 0.0
    for k in range(n_line):
        crossing[k].wait_recv()
        total = total + cross_in[k, line, :]
    share(1, total).wait_recv()
    out_p[...] = coupling(lambda k, rows: totals[1, k, rows, :])
    carried.wait_recv()
    for i, slot in enumerate((even, odd, odd)):
        move_copy(i, slot).wait_recv()
    for copy in pending:
        copy.wait_send()


def finish(work, p_ref, out_upper, out_lower, stage, sems):
    depth, width = out_upper.shape
    chunk = depth // STORES
    p = p_ref[...]
    d = work[0] - tall_dot(work[1], wide(p.T))
    p_wide, x_wide = wide(p), wide(2.0 * inverse_adaptive(p))
    copies = []
    for i in range(STORES):
        rows = pl.ds(i * chunk, chunk)
        y = turn(work[0, rows, :], work[1, rows, :], x_wide, p_wide, d[i * chunk : (i + 1) * chunk])
        for which, out in enumerate((out_upper, out_lower)):
            stage[which, rows, :] = y[which]
            copies.append(pltpu.make_async_copy(stage.at[which, rows], out.at[rows], sems.at[which, i]))
            copies[-1].start()
    for copy in copies:
        copy.wait()


def shards(n_row, n_col, upper_blocks, lower_blocks):
    depth, width = upper_blocks.shape
    half = width // 2
    n_line = n_row // 2
    out = jax.ShapeDtypeStruct((depth, width), F32)
    dma = pltpu.SemaphoreType.DMA
    flag = pltpu.SemaphoreType.REGULAR
    work, p = pl.pallas_call(
        functools.partial(kernel, n_row, n_col),
        out_shape=(pltpu.VMEM((3, depth, width), F32), pltpu.VMEM((width, width), F32)),
        in_specs=[pl.BlockSpec(memory_space=pl.ANY)] * 2,
        out_specs=(pl.BlockSpec(memory_space=pltpu.VMEM),) * 2,
        scratch_shapes=[
            pltpu.VMEM((2, depth, width), F32),
            pltpu.VMEM((2, RELAYED * (depth // 8), width), F32),
            pltpu.VMEM((2, depth, width), F32),
            pltpu.VMEM((3, depth, width), F32),
            pltpu.VMEM((ROUNDS, 2, half + 8, width), F32),
            pltpu.VMEM((2, half + 8, width), F32),
            pltpu.VMEM((ROUNDS, half + 8, width), F32),
            pltpu.VMEM((n_line - 1, half + 8, width), F32),
            pltpu.VMEM((n_line, half + 8, width), F32),
            pltpu.VMEM((ROUNDS, 2, half + 8, width), F32),
            pltpu.VMEM((2, half + 8, width), F32),
            pltpu.VMEM((2, half + 8, width), F32),
            dma((2,)),
            dma((2,)),
            dma((n_line - 1,)),
            dma((n_line - 1,)),
            dma((n_line,)),
            dma((n_line,)),
            dma((ROUNDS,)),
            dma((ROUNDS,)),
            dma((2,)),
            dma((2,)),
            dma((2,)),
            dma((2,)),
            dma((2, 2)),
            dma((2, 2)),
            dma((2, 2)),
            dma((2, 2)),
            dma((SHIFTS,)),
            dma((SHIFTS,)),
            dma((1,)),
            dma((1,)),
            dma((3,)),
            dma((3,)),
            dma((2, LOADS)),
            flag((max(n_line - 2, 1),)),
            flag((max(n_line - 2, 1),)),
        ],
        compiler_params=pltpu.CompilerParams(collective_id=0, has_side_effects=True),
    )(upper_blocks, lower_blocks)
    return pl.pallas_call(
        finish,
        out_shape=(out, out),
        in_specs=[pl.BlockSpec(memory_space=pltpu.VMEM)] * 2,
        out_specs=(pl.BlockSpec(memory_space=pl.ANY),) * 2,
        scratch_shapes=[pltpu.VMEM((2, depth, width), F32), dma((2, STORES))],
    )(*(pltpu.with_memory_space_constraint(x, pltpu.VMEM) for x in (work, p)))


def solution(mesh):
    placed = (P("row", "col"), P("row", "col"))
    return jax.shard_map(
        functools.partial(shards, mesh.shape["row"], mesh.shape["col"]),
        mesh=mesh,
        in_specs=placed,
        out_specs=(P("row", "col"), P("row", "col")),
        check_vma=False,
    )
```
